32 devices in a mesh: section: 2 (over core), expert: 16 (over z, y, x).
Axes of the slice: x: 2, y: 2, z: 4, core: 2. Of those that a mesh axis runs over, the one named last changes fastest.
Arguments:
- sent_forward: bfloat16 [2, 2048, 2048], P('section', 'expert'), may hold values from -6 to 6
- grad_sent: bfloat16 [2, 2048, 2048], P('section', 'expert'), may hold values from -1.796875 to 1.796875
- saved_inputs: bfloat16 [2, 2048, 2048], P('section', 'expert'), may hold values from -6 to 6
- routes_forward: int32 [2, 2048, 2], P('section', 'expert'), may hold values from 0 to 7, all different within a row; in each aligned block of 128 rows (0 to 127, 128 to 255, ..., all dimensions but the last counted through in order) at most 48 rows name the same one
- gates_forward: float32 [2, 2048, 2], P('section', 'expert'), may hold values from 0.1 to 1
- routes_backward: int32 [2, 2048, 2], P('section', 'expert'), may hold values from 0 to 7, all different within a row; in each aligned block of 128 rows (0 to 127, 128 to 255, ..., all dimensions but the last counted through in order) at most 48 rows name the same one
- gates_backward: float32 [2, 2048, 2], P('section', 'expert'), may hold values from 0.1 to 1
- w_gate: bfloat16 [2, 16, 2048, 384], P('section', 'expert'), may hold values from -0.125 to 0.125
- w_up: bfloat16 [2, 16, 2048, 384], P('section', 'expert'), may hold values from -0.125 to 0.125
- w_down: bfloat16 [2, 16, 384, 2048], P('section', 'expert'), may hold values from -0.21875 to 0.21875
Outputs:
- layer_out: bfloat16 [2, 2048, 2048], P('section', 'expert')
- grad_in: bfloat16 [2, 2048, 2048], P('section', 'expert')
- grad_gate: bfloat16 [2, 16, 2048, 384], P('section', 'expert')
- grad_up: bfloat16 [2, 16, 2048, 384], P('section', 'expert')
- grad_down: bfloat16 [2, 16, 384, 2048], P('section', 'expert')
The draws below stay inside these ranges and needn't reach their ends.
Inputs may be any that keep to these rules, and one draw needn't show every extreme that they name: `routes_forward`: each row names 2 different experts; among the 128 rows of one device no expert is named by more than 48 rows, and in some device's rows one expert is named by exactly 48. `routes_backward`: each row names 2 different experts; among the 128 rows of one device no expert is named by more than 48 rows, and in some device's rows one expert is named by exactly 48.
All inputs are finite; a program needn't handle non-finite values.
Results may differ from the reference program's by a relative error of at most 0.0065.
Values may be sent and summed in bfloat16 or wider, within the bound.
No kernel may reach another device: no remote copies, remote signals or barrier semaphores. Data moves between devices by JAX's collectives and lax.ppermute only.
A program may use at most 128 MiB of HBM per device.

```python
import math
import jax
import jax.numpy as jnp
import numpy as np
from jax import lax

D = 2048
FF = 768
TOPK = 2
TOK_DEV = 128
HID = 384
EXPERTS = 8
CAP = 48
TOK_SECTION = 2048
N_SECTION = 2
N_EXPERT = 16


def steps_of(own_key, shape, pieces, smallest, high):
    level, own = 1.0, jax.random.fold_in(own_key, 6)
    for dim, blocks in pieces:
        steps = jnp.exp(jax.random.uniform(jax.random.fold_in(own, dim), (blocks,), jnp.float32, smallest / len(pieces), high / len(pieces)))
        level = level * jnp.repeat(steps, shape[dim] // blocks).reshape([-1 if axis == dim else 1 for axis in range(len(shape))])
    return level


def shared_out(own_key, own, number, rows, count, top, bound, skew):
    sequence = jax.random.permutation(own_key, count)
    crowded, ordinary = portions_of(count, rows * top, bound, skew, True), portions_of(count, rows * top, bound, skew, False)
    places = jnp.arange(count)

    def named(tallies, rotation):
        used = int((tallies > 0).sum())
        fixed = max(1, used // 4)
        moved = fixed + (places - fixed + rotation * (used - fixed)) % max(1, count - fixed)
        return jnp.zeros((count,), jnp.int32).at[sequence[jnp.where(places < fixed, places, moved)]].set(jnp.asarray(tallies, jnp.int32))

    tallies = jnp.where(number % 4 == 0, named(crowded, number // 4), named(ordinary, number - number // 4 - 1))
    mixed = jax.random.permutation(jax.random.fold_in(own, 3), count)
    giver, taker = mixed[0:count // 2 * 2:2], mixed[1:count // 2 * 2:2]
    room = jnp.minimum(tallies[giver] - 1, bound - tallies[taker]) // 2
    room = jnp.where((giver == sequence[0]) | (taker == sequence[0]) | (tallies[taker] == 0), 0, jnp.maximum(room, 0))
    moved = jax.random.randint(jax.random.fold_in(own, 4), (count // 2,), 0, 1 << 20) % (room + 1)
    tallies = tallies.at[giver].add(-moved).at[taker].add(moved)
    labels = jnp.searchsorted(jnp.cumsum(tallies), jnp.arange(rows * top), side="right").astype(jnp.int32)
    grid = labels.reshape(top, rows).T
    grid = grid[jax.random.permutation(jax.random.fold_in(own, 1), rows)]
    rotation = jax.random.randint(jax.random.fold_in(own, 2), (rows, 1), 0, top)
    return jnp.take_along_axis(grid, (jnp.arange(top)[None, :] + rotation) % top, axis=1)


def portions_of(count, total, most, skew, full):
    loads = [(1 << 20) // math.isqrt(grade ** skew) + 1 for grade in range(1, count + 1)]
    largest = most if full else min(most, max(-(-total // count), total * loads[0] // sum(loads)))
    least = 1 if total - largest >= count - 1 else 0
    counts, spare = [largest] + [least] * (count - 1), total - largest - least * (count - 1)
    while spare > 0:
        candidates = [i for i in range(1, count) if counts[i] < largest] or [i for i in range(1, count) if counts[i] < most]
        whole, left = sum([loads[i] for i in candidates]), spare
        for i in candidates:
            extra = min(most - counts[i], max(1, left * loads[i] // whole), spare)
            counts[i] = counts[i] + extra
            spare = spare - extra
    return np.array(counts)


def gaussian(rng, shape, scale, bound, pieces=(), held_as=jnp.bfloat16):
    entries = scale * jax.random.normal(rng, shape, jnp.float32)
    if pieces:
        entries = entries * steps_of(rng, shape, pieces, -0.22, 0.18)
    return jnp.clip(entries, -bound, bound).astype(held_as)


def setup_inputs(seed: int = 0) -> dict:
    arg_keys = jax.random.split(jax.random.key(seed), 11)
    sent_forward = gaussian(arg_keys[0], (N_SECTION, TOK_SECTION, D), 1.0, 6.0, ((0, 2), (1, 16)))
    grad_sent = gaussian(arg_keys[1], (N_SECTION, TOK_SECTION, D), 0.3, 1.796875, ((0, 2), (1, 16)))
    saved_inputs = gaussian(arg_keys[2], (N_SECTION, TOK_SECTION, D), 1.0, 6.0, ((0, 2), (1, 16)))
    routes_forward_keys = jax.random.split(jax.random.fold_in(arg_keys[3], 1), N_SECTION * TOK_SECTION // TOK_DEV)
    routes_forward_turns = jax.random.permutation(jax.random.fold_in(arg_keys[3], 3), N_SECTION * TOK_SECTION // TOK_DEV)
    routes_forward = jax.vmap(lambda own, number: shared_out(jax.random.fold_in(arg_keys[3], 2), own, number, TOK_DEV, EXPERTS, TOPK, CAP, 2))(routes_forward_keys, routes_forward_turns).reshape((N_SECTION, TOK_SECTION, TOPK))
    gates_forward = jnp.clip(0.1 + 0.9 * jax.random.uniform(arg_keys[4], (N_SECTION, TOK_SECTION, TOPK), jnp.float32) ** steps_of(arg_keys[4], (N_SECTION, TOK_SECTION, TOPK), ((0, 2), (1, 16)), -0.2, 0.2), 0.1, 1.0)
    routes_backward_keys = jax.random.split(jax.random.fold_in(arg_keys[5], 1), N_SECTION * TOK_SECTION // TOK_DEV)
    routes_backward_turns = jax.random.permutation(jax.random.fold_in(arg_keys[5], 3), N_SECTION * TOK_SECTION // TOK_DEV)
    routes_backward = jax.vmap(lambda own, number: shared_out(jax.random.fold_in(arg_keys[5], 2), own, number, TOK_DEV, EXPERTS, TOPK, CAP, 2))(routes_backward_keys, routes_backward_turns).reshape((N_SECTION, TOK_SECTION, TOPK))
    gates_backward = jnp.clip(0.1 + 0.9 * jax.random.uniform(arg_keys[6], (N_SECTION, TOK_SECTION, TOPK), jnp.float32) ** steps_of(arg_keys[6], (N_SECTION, TOK_SECTION, TOPK), ((0, 2), (1, 16)), -0.2, 0.2), 0.1, 1.0)
    w_gate = gaussian(arg_keys[7], (N_SECTION, N_EXPERT, D, HID), D ** -0.5, 0.125, ((0, 2), (1, 16)))
    w_up = gaussian(arg_keys[8], (N_SECTION, N_EXPERT, D, HID), D ** -0.5, 0.125, ((0, 2), (1, 16)))
    w_down = gaussian(arg_keys[9], (N_SECTION, N_EXPERT, HID, D), FF ** -0.5, 0.21875, ((0, 2), (1, 16)))
    return {"sent_forward": sent_forward, "grad_sent": grad_sent, "saved_inputs": saved_inputs, "routes_forward": routes_forward, "gates_forward": gates_forward, "routes_backward": routes_backward, "gates_backward": gates_backward, "w_gate": w_gate, "w_up": w_up, "w_down": w_down}


def route_tables(routes, gates, experts, capacity):
    tokens = routes.shape[0]
    chosen = routes.shape[1]
    flat_ids = routes.reshape(-1).astype(jnp.int32)
    hits = (flat_ids[:, None] == jnp.arange(experts, dtype=jnp.int32)[None, :]).astype(jnp.int32)
    earlier = jnp.cumsum(hits, axis=0) - hits
    slot_ids = jnp.sum(earlier * hits, axis=1).astype(jnp.int32)
    target = (flat_ids * capacity + slot_ids).astype(jnp.int32)
    placed = (target[:, None] == jnp.arange(experts * capacity, dtype=jnp.int32)[None, :]).astype(jnp.float32)
    placed = placed.reshape(tokens, chosen, experts * capacity)
    dispatch = jnp.sum(placed, axis=1)
    combine = jnp.sum(placed * gates[:, :, None].astype(jnp.float32), axis=1)
    return dispatch, combine


def gather_rows(dispatch, values):
    return lax.dot_general(dispatch.astype(jnp.bfloat16), values, (((0,), (0,)), ((), ())),
                           preferred_element_type=jnp.float32).astype(jnp.bfloat16)


def scale_rows(combine, values):
    return lax.dot_general(combine, values.astype(jnp.float32), (((0,), (0,)), ((), ())),
                           precision=lax.Precision.HIGHEST,
                           preferred_element_type=jnp.float32).astype(jnp.bfloat16)


def mix_rows(table, slot_values):
    return jnp.dot(table, slot_values, precision=lax.Precision.HIGHEST, preferred_element_type=jnp.float32)


def half_forward(inputs, gate_matrix, up_matrix, down_matrix):
    gate_act = jnp.dot(inputs, gate_matrix, preferred_element_type=jnp.float32)
    up_act = jnp.dot(inputs, up_matrix, preferred_element_type=jnp.float32)
    hidden = (gate_act * jax.nn.sigmoid(gate_act) * up_act).astype(jnp.bfloat16)
    return jnp.dot(hidden, down_matrix, preferred_element_type=jnp.float32).astype(jnp.bfloat16)


def slot_half(values, half):
    width = values.shape[-1]
    return values.reshape(N_EXPERT, 2, CAP // 2, width)[:, half].reshape(-1, width)


def rounded_pair(lower, upper):
    lower_r = lax.optimization_barrier(lower.astype(jnp.bfloat16)).astype(jnp.float32)
    upper_r = lax.optimization_barrier(upper.astype(jnp.bfloat16)).astype(jnp.float32)
    return lower_r + upper_r


def half_backward(inputs, upstream, gate_matrix, up_matrix, down_matrix):
    gate_act = jnp.dot(inputs, gate_matrix, preferred_element_type=jnp.float32)
    up_act = jnp.dot(inputs, up_matrix, preferred_element_type=jnp.float32)
    sigma = jax.nn.sigmoid(gate_act)
    swish = gate_act * sigma
    hidden = (swish * up_act).astype(jnp.bfloat16)
    inner = (((1,), (1,)), ((), ()))
    outer = (((0,), (0,)), ((), ()))
    d_hidden = lax.dot_general(upstream, down_matrix, inner, preferred_element_type=jnp.float32)
    d_gate = (d_hidden * up_act * sigma * (1.0 + gate_act * (1.0 - sigma))).astype(jnp.bfloat16)
    d_up = (d_hidden * swish).astype(jnp.bfloat16)
    terms = []
    for half in range(2):
        rows_in = slot_half(inputs, half)
        terms.append((
            lax.dot_general(rows_in, slot_half(d_gate, half), outer, preferred_element_type=jnp.float32),
            lax.dot_general(rows_in, slot_half(d_up, half), outer, preferred_element_type=jnp.float32),
            lax.dot_general(slot_half(hidden, half), slot_half(upstream, half), outer,
                            preferred_element_type=jnp.float32)))
    grad_gate = rounded_pair(terms[0][0], terms[1][0])
    grad_up = rounded_pair(terms[0][1], terms[1][1])
    grad_down = rounded_pair(terms[0][2], terms[1][2])
    back = lax.dot_general(d_gate, gate_matrix, inner, preferred_element_type=jnp.float32)
    back = back + lax.dot_general(d_up, up_matrix, inner, preferred_element_type=jnp.float32)
    return back.astype(jnp.bfloat16), grad_gate, grad_up, grad_down


def reference(sent_forward, grad_sent, saved_inputs, routes_forward, gates_forward, routes_backward,
              gates_backward, w_gate, w_up, w_down):
    experts = N_EXPERT // 2
    capacity = CAP

    def make_tables(routes, gates):
        return route_tables(routes, gates, experts, capacity)

    def by_expert(values):
        return values.reshape(N_EXPERT, experts, capacity, D).transpose(1, 0, 2, 3).reshape(experts, N_EXPERT * capacity, D)

    def by_block(values):
        return values.reshape(experts, N_EXPERT, capacity, D).transpose(1, 0, 2, 3).reshape(N_EXPERT, experts * capacity, D)

    def per_expert(packed):
        rows_forward, rows_backward, rows_grad, gate_pair, up_pair, down_pair = packed
        parts = []
        backs = []
        grads_g = []
        grads_u = []
        grads_d = []
        for half in range(2):
            parts.append(half_forward(rows_forward, gate_pair[half], up_pair[half], down_pair[half]))
            back, g_gate, g_up, g_down = half_backward(rows_backward, rows_grad, gate_pair[half], up_pair[half], down_pair[half])
            backs.append(back)
            grads_g.append(g_gate)
            grads_u.append(g_up)
            grads_d.append(g_down)
        return (jnp.stack(parts), jnp.stack(backs), jnp.stack(grads_g), jnp.stack(grads_u), jnp.stack(grads_d))

    outputs = []
    input_grads = []
    gate_grads = []
    up_grads = []
    down_grads = []
    for section_index in range(N_SECTION):
        arrived = sent_forward[(section_index - 1) % N_SECTION].reshape(N_EXPERT, TOK_DEV, D)
        returned = grad_sent[(section_index + 1) % N_SECTION].reshape(N_EXPERT, TOK_DEV, D)
        saved = saved_inputs[section_index].reshape(N_EXPERT, TOK_DEV, D)
        dispatch_forward, combine_forward = jax.vmap(make_tables)(
            routes_forward[section_index].reshape(N_EXPERT, TOK_DEV, TOPK),
            gates_forward[section_index].reshape(N_EXPERT, TOK_DEV, TOPK))
        dispatch_backward, combine_backward = jax.vmap(make_tables)(
            routes_backward[section_index].reshape(N_EXPERT, TOK_DEV, TOPK),
            gates_backward[section_index].reshape(N_EXPERT, TOK_DEV, TOPK))
        slots_forward = by_expert(jax.vmap(gather_rows)(dispatch_forward, arrived))
        slots_backward = by_expert(jax.vmap(gather_rows)(dispatch_backward, saved))
        slots_grad = by_expert(jax.vmap(scale_rows)(combine_backward, returned))
        gate_pairs = w_gate[section_index].reshape(experts, 2, D, HID)
        up_pairs = w_up[section_index].reshape(experts, 2, D, HID)
        down_pairs = w_down[section_index].reshape(experts, 2, HID, D)
        results = lax.map(per_expert, (slots_forward, slots_backward, slots_grad, gate_pairs, up_pairs, down_pairs))
        summed_out = by_block(jnp.sum(results[0].astype(jnp.float32), axis=1))
        summed_back = by_block(jnp.sum(results[1].astype(jnp.float32), axis=1))
        section_out = jax.vmap(mix_rows)(combine_forward, summed_out)
        section_back = jax.vmap(mix_rows)(dispatch_backward, summed_back)
        outputs.append(section_out.astype(jnp.bfloat16).reshape(TOK_SECTION, D))
        input_grads.append(section_back.astype(jnp.bfloat16).reshape(TOK_SECTION, D))
        gate_grads.append(results[2].reshape(N_EXPERT, D, HID).astype(jnp.bfloat16))
        up_grads.append(results[3].reshape(N_EXPERT, D, HID).astype(jnp.bfloat16))
        down_grads.append(results[4].reshape(N_EXPERT, HID, D).astype(jnp.bfloat16))
    return (jnp.stack(outputs), jnp.stack(input_grads), jnp.stack(gate_grads), jnp.stack(up_grads), jnp.stack(down_grads))
```

```python
import functools

import jax
import jax.numpy as jnp
from jax import lax
from jax.experimental import pallas as pl
from jax.experimental.pallas import tpu as pltpu
from jax.sharding import PartitionSpec as P

VMEM_LIMIT = 48 << 20


def whole(n):
    return [pl.BlockSpec(memory_space=pltpu.VMEM)] * n


def params():
    return pltpu.CompilerParams(vmem_limit_bytes=VMEM_LIMIT)


def placement(me, routes, experts, capacity):
    tokens = routes.shape[1]
    rel = lax.bitwise_xor(routes, me)
    expert_row = lax.broadcasted_iota(jnp.int32, (experts, tokens), 0)
    first = rel[0:1, :] == expert_row
    second = rel[1:2, :] == expert_row
    hits = (first | second).astype(jnp.bfloat16)
    before = lax.broadcasted_iota(jnp.int32, (tokens, tokens), 0) < lax.broadcasted_iota(
        jnp.int32, (tokens, tokens), 1
    )
    earlier = jnp.dot(hits, before.astype(jnp.bfloat16), preferred_element_type=jnp.float32)
    slot0 = jnp.sum(jnp.where(first, earlier, 0.0), axis=0, keepdims=True).astype(jnp.int32)
    slot1 = jnp.sum(jnp.where(second, earlier, 0.0), axis=0, keepdims=True).astype(jnp.int32)
    place = lax.broadcasted_iota(jnp.int32, (experts * capacity, tokens), 0)
    at0 = place == rel[0:1, :] * capacity + slot0
    at1 = place == rel[1:2, :] * capacity + slot1
    return at0, at1


def as_bf16(mask):
    return mask.astype(jnp.float32).astype(jnp.bfloat16)


def dispatch_kernel(experts, capacity, scaled, me_ref, routes_ref, *refs):
    if scaled:
        gates_ref, values_ref, *out_refs = refs
    else:
        values_ref, *out_refs = refs
    at0, at1 = placement(me_ref[0], routes_ref[...], experts, capacity)
    picked = jnp.dot(as_bf16(at0 | at1), values_ref[...], preferred_element_type=jnp.float32)
    if scaled:
        gate = jnp.where(at0, gates_ref[0:1, :], 0.0) + jnp.where(at1, gates_ref[1:2, :], 0.0)
        picked = picked * jnp.sum(gate, axis=1, keepdims=True)
    picked = picked.astype(jnp.bfloat16)
    for i, out in enumerate(out_refs):
        out[...] = picked[i * capacity : (i + 1) * capacity, :]


def dispatch(me, routes, values, experts, capacity, gates=None):
    width = values.shape[1]
    operands = (me, routes) + (() if gates is None else (gates,)) + (values,)
    return pl.pallas_call(
        functools.partial(dispatch_kernel, experts, capacity, gates is not None),
        out_shape=[jax.ShapeDtypeStruct((capacity, width), jnp.bfloat16)] * experts,
        in_specs=[pl.BlockSpec(memory_space=pltpu.SMEM)] + whole(len(operands) - 1),
        out_specs=whole(experts),
        compiler_params=params(),
        cost_estimate=pl.CostEstimate(
            flops=2 * experts * capacity * values.size,
            bytes_accessed=2 * (values.size + experts * capacity * width),
            transcendentals=0,
        ),
        name="dispatch",
    )(*operands)


def combine_kernel(experts, capacity, scaled, me_ref, routes_ref, *refs):
    if scaled:
        gates_ref, *refs = refs
    *in_refs, out_ref, rows = refs
    for i, ref in enumerate(in_refs):
        rows[i * capacity : (i + 1) * capacity, :] = ref[...]
    at0, at1 = placement(me_ref[0], routes_ref[...], experts, capacity)
    outer = (((0,), (0,)), ((), ()))

    def pick(table):
        return lax.dot_general(
            table, rows[...], outer, preferred_element_type=jnp.float32
        )

    if scaled:
        gate = jnp.where(at0, gates_ref[0:1, :], 0.0) + jnp.where(at1, gates_ref[1:2, :], 0.0)
        high = gate.astype(jnp.bfloat16)
        low = (gate - high.astype(jnp.float32)).astype(jnp.bfloat16)
        out_ref[...] = (pick(high) + pick(low)).astype(jnp.bfloat16)
    else:
        out_ref[...] = pick(as_bf16(at0 | at1)).astype(jnp.bfloat16)


def combine(me, routes, pieces, experts, capacity, gates=None):
    width = pieces[0].shape[1]
    tokens = routes.shape[1]
    operands = (me, routes) + (() if gates is None else (gates,)) + tuple(pieces)
    return pl.pallas_call(
        functools.partial(combine_kernel, experts, capacity, gates is not None),
        out_shape=jax.ShapeDtypeStruct((tokens, width), jnp.bfloat16),
        in_specs=[pl.BlockSpec(memory_space=pltpu.SMEM)] + whole(len(operands) - 1),
        out_specs=pl.BlockSpec(memory_space=pltpu.VMEM),
        scratch_shapes=[pltpu.VMEM((experts * capacity, width), jnp.bfloat16)],
        compiler_params=params(),
        cost_estimate=pl.CostEstimate(
            flops=2 * tokens * experts * capacity * width,
            bytes_accessed=2 * (tokens * width + experts * capacity * width),
            transcendentals=0,
        ),
        name="combine",
    )(*operands)


def forward_kernel(pieces, capacity, *refs):
    in_refs = refs[:pieces]
    gate_ref, up_ref, down_ref = refs[pieces : pieces + 3]
    out_refs = refs[pieces + 3 : 2 * pieces + 3]
    rows = refs[-1]
    for i, ref in enumerate(in_refs):
        rows[i * capacity : (i + 1) * capacity, :] = ref[...]
    gate_act = jnp.dot(rows[...], gate_ref[...], preferred_element_type=jnp.float32)
    up_act = jnp.dot(rows[...], up_ref[...], preferred_element_type=jnp.float32)
    hidden = (gate_act * jax.nn.sigmoid(gate_act) * up_act).astype(jnp.bfloat16)
    part = jnp.dot(hidden, down_ref[...], preferred_element_type=jnp.float32).astype(jnp.bfloat16)
    for i, out in enumerate(out_refs):
        out[...] = part[i * capacity : (i + 1) * capacity, :]


def forward_half(pieces, gate, up, down):
    n = len(pieces)
    capacity, width = pieces[0].shape
    hidden = gate.shape[1]
    return pl.pallas_call(
        functools.partial(forward_kernel, n, capacity),
        out_shape=[jax.ShapeDtypeStruct((capacity, width), jnp.bfloat16)] * n,
        in_specs=whole(n + 3),
        out_specs=whole(n),
        scratch_shapes=[pltpu.VMEM((n * capacity, width), jnp.bfloat16)],
        compiler_params=params(),
        cost_estimate=pl.CostEstimate(
            flops=6 * n * capacity * width * hidden,
            bytes_accessed=4 * n * capacity * width + 6 * width * hidden,
            transcendentals=n * capacity * hidden,
        ),
        name="forward_half",
    )(*pieces, gate, up, down)


def backward_kernel(pieces, capacity, *refs):
    in_refs = refs[:pieces]
    up_refs = refs[pieces : 2 * pieces]
    gate_ref, up_ref, down_ref = refs[2 * pieces : 2 * pieces + 3]
    out_refs = refs[2 * pieces + 3 : 3 * pieces + 3]
    hidden_ref, d_gate_ref, d_up_ref, rows, upstream = refs[3 * pieces + 3 :]
    for i in range(pieces):
        rows[i * capacity : (i + 1) * capacity, :] = in_refs[i][...]
        upstream[i * capacity : (i + 1) * capacity, :] = up_refs[i][...]
    inner = (((1,), (1,)), ((), ()))
    gate_act = jnp.dot(rows[...], gate_ref[...], preferred_element_type=jnp.float32)
    up_act = jnp.dot(rows[...], up_ref[...], preferred_element_type=jnp.float32)
    d_hidden = lax.dot_general(
        upstream[...], down_ref[...], inner, preferred_element_type=jnp.float32
    )
    sigma = jax.nn.sigmoid(gate_act)
    swish = gate_act * sigma
    hidden_ref[...] = (swish * up_act).astype(jnp.bfloat16)
    d_gate = (d_hidden * up_act * sigma * (1.0 + gate_act * (1.0 - sigma))).astype(jnp.bfloat16)
    d_up = (d_hidden * swish).astype(jnp.bfloat16)
    d_gate_ref[...] = d_gate
    d_up_ref[...] = d_up
    back = lax.dot_general(d_gate, gate_ref[...], inner, preferred_element_type=jnp.float32)
    back = back + lax.dot_general(d_up, up_ref[...], inner, preferred_element_type=jnp.float32)
    back = back.astype(jnp.bfloat16)
    for i, out in enumerate(out_refs):
        out[...] = back[i * capacity : (i + 1) * capacity, :]


def backward_half(pieces, upstream, gate, up, down):
    n = len(pieces)
    capacity, width = pieces[0].shape
    hidden = gate.shape[1]
    small = jax.ShapeDtypeStruct((n * capacity, hidden), jnp.bfloat16)
    out = pl.pallas_call(
        functools.partial(backward_kernel, n, capacity),
        out_shape=[jax.ShapeDtypeStruct((capacity, width), jnp.bfloat16)] * n + [small] * 3,
        in_specs=whole(2 * n + 3),
        out_specs=whole(n + 3),
        scratch_shapes=[pltpu.VMEM((n * capacity, width), jnp.bfloat16)] * 2,
        compiler_params=params(),
        cost_estimate=pl.CostEstimate(
            flops=10 * n * capacity * width * hidden,
            bytes_accessed=6 * n * capacity * width + 6 * width * hidden,
            transcendentals=n * capacity * hidden,
        ),
        name="backward_half",
    )(*pieces, *upstream, gate, up, down)
    return out[:n], out[n], out[n + 1], out[n + 2]


def add_pair(a, b):
    return (a.astype(jnp.float32) + b.astype(jnp.float32)).astype(jnp.bfloat16)


def per_device(
    sent_forward,
    grad_sent,
    saved_inputs,
    routes_forward,
    gates_forward,
    routes_backward,
    gates_backward,
    w_gate,
    w_up,
    w_down,
):
    devices = lax.axis_size("expert")
    experts = devices // 2
    sections = lax.axis_size("section")
    tokens = sent_forward.shape[1]
    chosen = routes_forward.shape[2]
    capacity = 3 * tokens * chosen // (2 * experts)
    me = (lax.axis_index("expert") // 2).astype(jnp.int32).reshape(1)

    def along(array, by):
        return lax.ppermute(array, "section", [(i, (i + by) % sections) for i in range(sections)])

    def to_xor(array, mask):
        return lax.ppermute(array, "expert", [(i, i ^ mask) for i in range(devices)])

    def spread(pieces):
        own = [pieces[0]] + [to_xor(pieces[d], 2 * d) for d in range(1, experts)]
        other = [to_xor(piece, 1) for piece in own]
        return own, other

    def gather_back(own, other):
        summed = [add_pair(own[d], to_xor(other[d], 1)) for d in range(experts)]
        return [summed[0]] + [to_xor(summed[d], 2 * d) for d in range(1, experts)]

    routes_f, gates_f = routes_forward[0].T, gates_forward[0].T
    routes_b, gates_b = routes_backward[0].T, gates_backward[0].T
    own_gate, own_up, own_down = w_gate[0, 0], w_up[0, 0], w_down[0, 0]

    slots_x = dispatch(me, routes_b, saved_inputs[0], experts, capacity)
    returned = along(grad_sent, -1)[0]
    slots_g = dispatch(me, routes_b, returned, experts, capacity, gates_b)
    arrived = along(sent_forward, 1)[0]
    slots_f = dispatch(me, routes_f, arrived, experts, capacity)

    x_own, x_other = spread(slots_x)
    g_own, g_other = spread(slots_g)
    f_own, f_other = spread(slots_f)

    back_own, hid_own, dg_own, du_own = backward_half(x_own, g_own, own_gate, own_up, own_down)
    back_other, hid_other, dg_other, du_other = backward_half(
        x_other, g_other, own_gate, own_up, own_down
    )
    back = gather_back(back_own, back_other)

    out_own = forward_half(f_own, own_gate, own_up, own_down)
    out_other = forward_half(f_other, own_gate, own_up, own_down)
    out = gather_back(out_own, out_other)

    inputs = jnp.concatenate(list(x_own) + list(x_other))
    upstream = jnp.concatenate(list(g_own) + list(g_other))
    hidden = jnp.concatenate([hid_own, hid_other])
    d_gate = jnp.concatenate([dg_own, dg_other])
    d_up = jnp.concatenate([du_own, du_other])
    outer = (((0,), (0,)), ((), ()))

    def weight_term(a, b):
        return lax.dot_general(a, b, outer, preferred_element_type=jnp.float32).astype(jnp.bfloat16)

    grad_gate = weight_term(inputs, d_gate)
    grad_up = weight_term(inputs, d_up)
    grad_down = weight_term(hidden, upstream)

    grad_in = combine(me, routes_b, back, experts, capacity)
    layer_out = combine(me, routes_f, out, experts, capacity, gates_f)
    return (
        layer_out[None],
        grad_in[None],
        grad_gate[None, None],
        grad_up[None, None],
        grad_down[None, None],
    )


def solution(mesh):
    rows = P("section", "expert", None)
    weights = P("section", "expert", None, None)
    return jax.shard_map(
        per_device,
        mesh=mesh,
        in_specs=(rows,) * 7 + (weights,) * 3,
        out_specs=(rows, rows, weights, weights, weights),
        check_vma=False,
    )
```

```python
import functools

import jax
import jax.numpy as jnp
from jax import lax
from jax.experimental import pallas as pl
from jax.experimental.pallas import tpu as pltpu
from jax.sharding import PartitionSpec as P

VMEM_LIMIT = 48 << 20


def whole(n):
    return [pl.BlockSpec(memory_space=pltpu.VMEM)] * n


def params():
    return pltpu.CompilerParams(vmem_limit_bytes=VMEM_LIMIT)


def placement(me, routes, experts, capacity):
    tokens = routes.shape[1]
    rel = lax.bitwise_xor(routes, me)
    expert_row = lax.broadcasted_iota(jnp.int32, (experts, tokens), 0)
    first = rel[0:1, :] == expert_row
    second = rel[1:2, :] == expert_row
    hits = (first | second).astype(jnp.bfloat16)
    before = lax.broadcasted_iota(jnp.int32, (tokens, tokens), 0) < lax.broadcasted_iota(
        jnp.int32, (tokens, tokens), 1
    )
    earlier = jnp.dot(hits, before.astype(jnp.bfloat16), preferred_element_type=jnp.float32)
    slot0 = jnp.sum(jnp.where(first, earlier, 0.0), axis=0, keepdims=True).astype(jnp.int32)
    slot1 = jnp.sum(jnp.where(second, earlier, 0.0), axis=0, keepdims=True).astype(jnp.int32)
    place = lax.broadcasted_iota(jnp.int32, (experts * capacity, tokens), 0)
    at0 = place == rel[0:1, :] * capacity + slot0
    at1 = place == rel[1:2, :] * capacity + slot1
    return at0, at1


def as_bf16(mask):
    return mask.astype(jnp.float32).astype(jnp.bfloat16)


def dispatch_kernel(experts, capacity, me_ref, routes_ref, *refs):
    out_refs = refs[-experts:]
    at0, at1 = placement(me_ref[0], routes_ref[...], experts, capacity)
    table = as_bf16(at0 | at1)
    picked = jnp.dot(table, refs[0][...], preferred_element_type=jnp.float32).astype(jnp.bfloat16)
    for i, out in enumerate(out_refs):
        out[0:capacity, :] = picked[i * capacity : (i + 1) * capacity, :]
    if len(refs) == experts + 3:
        gates_ref, upstream_ref = refs[1:3]
        gate = jnp.where(at0, gates_ref[0:1, :], 0.0) + jnp.where(at1, gates_ref[1:2, :], 0.0)
        scaled = jnp.dot(table, upstream_ref[...], preferred_element_type=jnp.float32)
        scaled = (scaled * jnp.sum(gate, axis=1, keepdims=True)).astype(jnp.bfloat16)
        for i, out in enumerate(out_refs):
            out[capacity:, :] = scaled[i * capacity : (i + 1) * capacity, :]


def dispatch(me, routes, values, experts, capacity, gates=None, upstream=None):
    width = values.shape[1]
    many = 1 if gates is None else 2
    operands = (me, routes, values) + (() if gates is None else (gates, upstream))
    return pl.pallas_call(
        functools.partial(dispatch_kernel, experts, capacity),
        out_shape=[jax.ShapeDtypeStruct((many * capacity, width), jnp.bfloat16)] * experts,
        in_specs=[pl.BlockSpec(memory_space=pltpu.SMEM)] + whole(len(operands) - 1),
        out_specs=whole(experts),
        compiler_params=params(),
        cost_estimate=pl.CostEstimate(
            flops=2 * many * experts * capacity * values.size,
            bytes_accessed=2 * many * (values.size + experts * capacity * width),
            transcendentals=0,
        ),
        name="dispatch",
    )(*operands)


def combine_kernel(experts, capacity, scaled, me_ref, routes_ref, *refs):
    if scaled:
        gates_ref, *refs = refs
    *in_refs, out_ref, rows = refs
    for i, ref in enumerate(in_refs):
        rows[i * capacity : (i + 1) * capacity, :] = ref[...]
    at0, at1 = placement(me_ref[0], routes_ref[...], experts, capacity)
    outer = (((0,), (0,)), ((), ()))

    def pick(table):
        return lax.dot_general(
            table, rows[...], outer, preferred_element_type=jnp.float32
        )

    if scaled:
        gate = jnp.where(at0, gates_ref[0:1, :], 0.0) + jnp.where(at1, gates_ref[1:2, :], 0.0)
        high = gate.astype(jnp.bfloat16)
        low = (gate - high.astype(jnp.float32)).astype(jnp.bfloat16)
        out_ref[...] = (pick(high) + pick(low)).astype(jnp.bfloat16)
    else:
        out_ref[...] = pick(as_bf16(at0 | at1)).astype(jnp.bfloat16)


def combine(me, routes, pieces, experts, capacity, gates=None):
    width = pieces[0].shape[1]
    tokens = routes.shape[1]
    operands = (me, routes) + (() if gates is None else (gates,)) + tuple(pieces)
    return pl.pallas_call(
        functools.partial(combine_kernel, experts, capacity, gates is not None),
        out_shape=jax.ShapeDtypeStruct((tokens, width), jnp.bfloat16),
        in_specs=[pl.BlockSpec(memory_space=pltpu.SMEM)] + whole(len(operands) - 1),
        out_specs=pl.BlockSpec(memory_space=pltpu.VMEM),
        scratch_shapes=[pltpu.VMEM((experts * capacity, width), jnp.bfloat16)],
        compiler_params=params(),
        cost_estimate=pl.CostEstimate(
            flops=2 * tokens * experts * capacity * width,
            bytes_accessed=2 * (tokens * width + experts * capacity * width),
            transcendentals=0,
        ),
        name="combine",
    )(*operands)


def put(out_refs, values, order):
    step, at, places = values.shape[0] // len(order), 0, {}
    for out in out_refs:
        for row in range(0, out.shape[0], step):
            places[at] = (out, row)
            at += 1
    for n, i in enumerate(order):
        out, row = places[i]
        out[row : row + step, :] = values[n * step : (n + 1) * step, :]


def forward_kernel(pieces, outs, order, *refs):
    in_refs = refs[:pieces]
    gate_ref, up_ref, down_ref = refs[pieces : pieces + 3]
    out_refs = refs[pieces + 3 : pieces + 3 + outs]
    rows = refs[-1]
    at = 0
    for ref in in_refs:
        rows[at : at + ref.shape[0], :] = ref[...]
        at += ref.shape[0]
    gate_act = jnp.dot(rows[...], gate_ref[...], preferred_element_type=jnp.float32)
    up_act = jnp.dot(rows[...], up_ref[...], preferred_element_type=jnp.float32)
    hidden = (gate_act * jax.nn.sigmoid(gate_act) * up_act).astype(jnp.bfloat16)
    part = jnp.dot(hidden, down_ref[...], preferred_element_type=jnp.float32).astype(jnp.bfloat16)
    put(out_refs, part, order)


def forward_half(pieces, gate, up, down, outs, order=None):
    n = len(pieces)
    total = sum(piece.shape[0] for piece in pieces)
    width, hidden = gate.shape
    return pl.pallas_call(
        functools.partial(forward_kernel, n, len(outs), order or range(8)),
        out_shape=[jax.ShapeDtypeStruct((rows, width), jnp.bfloat16) for rows in outs],
        in_specs=whole(n + 3),
        out_specs=whole(len(outs)),
        scratch_shapes=[pltpu.VMEM((total, width), jnp.bfloat16)],
        compiler_params=params(),
        cost_estimate=pl.CostEstimate(
            flops=6 * total * width * hidden,
            bytes_accessed=4 * total * width + 6 * width * hidden,
            transcendentals=total * hidden,
        ),
        name="forward_half",
    )(*pieces, gate, up, down)


def backward_kernel(pieces, outs, *refs):
    in_refs = refs[:pieces]
    gate_ref, up_ref, down_ref = refs[pieces : pieces + 3]
    out_refs = refs[pieces + 3 : pieces + 3 + outs]
    hidden_ref, d_gate_ref, d_up_ref, rows, upstream = refs[pieces + 3 + outs :]
    half = in_refs[0].shape[0] // 2
    for i, ref in enumerate(in_refs):
        rows[i * half : (i + 1) * half, :] = ref[0:half, :]
        upstream[i * half : (i + 1) * half, :] = ref[half:, :]
    inner = (((1,), (1,)), ((), ()))
    gate_act = jnp.dot(rows[...], gate_ref[...], preferred_element_type=jnp.float32)
    up_act = jnp.dot(rows[...], up_ref[...], preferred_element_type=jnp.float32)
    d_hidden = lax.dot_general(
        upstream[...], down_ref[...], inner, preferred_element_type=jnp.float32
    )
    sigma = jax.nn.sigmoid(gate_act)
    swish = gate_act * sigma
    hidden_ref[...] = (swish * up_act).astype(jnp.bfloat16)
    d_gate = (d_hidden * up_act * sigma * (1.0 + gate_act * (1.0 - sigma))).astype(jnp.bfloat16)
    d_up = (d_hidden * swish).astype(jnp.bfloat16)
    d_gate_ref[...] = d_gate
    d_up_ref[...] = d_up
    back = lax.dot_general(d_gate, gate_ref[...], inner, preferred_element_type=jnp.float32)
    back = back + lax.dot_general(d_up, up_ref[...], inner, preferred_element_type=jnp.float32)
    back = back.astype(jnp.bfloat16)
    put(out_refs, back, range(8))


def backward_half(pieces, gate, up, down, outs):
    n = len(pieces)
    total = sum(piece.shape[0] for piece in pieces) // 2
    width, hidden = gate.shape
    small = jax.ShapeDtypeStruct((total, hidden), jnp.bfloat16)
    large = jax.ShapeDtypeStruct((total, width), jnp.bfloat16)
    out = pl.pallas_call(
        functools.partial(backward_kernel, n, len(outs)),
        out_shape=[jax.ShapeDtypeStruct((rows, width), jnp.bfloat16) for rows in outs]
        + [small] * 3
        + [large] * 2,
        in_specs=whole(n + 3),
        out_specs=whole(len(outs) + 5),
        compiler_params=params(),
        cost_estimate=pl.CostEstimate(
            flops=10 * total * width * hidden,
            bytes_accessed=10 * total * width + 6 * width * hidden,
            transcendentals=total * hidden,
        ),
        name="backward_half",
    )(*pieces, gate, up, down)
    return out[: len(outs)], out[len(outs) :]


def add_pair(a, b):
    return (a.astype(jnp.float32) + b.astype(jnp.float32)).astype(jnp.bfloat16)


def per_device(
    sent_forward,
    grad_sent,
    saved_inputs,
    routes_forward,
    gates_forward,
    routes_backward,
    gates_backward,
    w_gate,
    w_up,
    w_down,
):
    devices = lax.axis_size("expert")
    experts = devices // 2
    sections = lax.axis_size("section")
    tokens = sent_forward.shape[1]
    chosen = routes_forward.shape[2]
    capacity = 3 * tokens * chosen // (2 * experts)
    me = (lax.axis_index("expert") // 2).astype(jnp.int32).reshape(1)

    def along(array, by):
        return lax.ppermute(array, "section", [(i, (i + by) % sections) for i in range(sections)])

    def to_xor(array, mask):
        return lax.ppermute(array, "expert", [(i, i ^ mask) for i in range(devices)])

    routes_f, gates_f = routes_forward[0].T, gates_forward[0].T
    routes_b, gates_b = routes_backward[0].T, gates_backward[0].T
    weights = w_gate[0, 0], w_up[0, 0], w_down[0, 0]
    span = experts // 8
    group = [list(range(i * span, (i + 1) * span)) for i in range(8)]
    lump = span * capacity
    split = [lump, lump, 2 * lump, 2 * lump, 2 * lump]

    held, met, rounds = {}, [], []

    def after_met(array):
        return lax.optimization_barrier((array, *met))[0] if met else array

    def start(name, arrays, masks):
        held[name] = [
            to_xor(after_met(a), m) if m else a for a, m in zip(arrays, masks, strict=True)
        ]

    def meet(*names):
        met[:] = [a for name in names for a in held[name]]
        rounds.append(list(met))

    def z_start(kind, slots, i):
        start((kind, i), [slots[d] for d in group[i]], [2 * d for d in group[i]])

    def x_start(i):
        start(("x", i), held["b", i], [1] * span)

    def x_join(q, members):
        rows = [a for i in members for a in held["f", i]]
        start(("fx", q), [jnp.concatenate(rows) if len(rows) > 1 else rows[0]], [1])

    def part_start(kind, parts, q):
        start((kind, q), [parts[q + 1]], [1])

    def both_start(i):
        start(("bx", i), [jnp.concatenate([back_other[i], out_other[i]])], [1])

    def give_back(kind, own, i):
        q, first = i // 2, (i % 2) * span
        both = []
        for n in range(span):
            rows = slice((first + n) * capacity, (first + n + 1) * capacity)
            both.append(add_pair(own[q + 1][rows], held[kind + "x", q][0][rows]))
        start((kind, i), both, [2 * d for d in group[i]])

    def give_both(i):
        both = []
        for n in range(span):
            own_rows = slice(n * capacity, (n + 1) * capacity)
            met_rows = slice(lump + n * capacity, lump + (n + 1) * capacity)
            pair = [
                add_pair(back_own[i][own_rows], held["bx", i][0][own_rows]),
                add_pair(out_own[i][own_rows], held["bx", i][0][met_rows]),
            ]
            both.append(jnp.concatenate(pair))
        start(("both", i), both, [2 * d for d in group[i]])
        held["r", i] = [a[:capacity] for a in held["both", i]]
        held["o", i] = [a[capacity:] for a in held["both", i]]

    returned = along(grad_sent, -1)[0]
    arrived = along(sent_forward, 1)[0]
    slots_b = dispatch(me, routes_b, saved_inputs[0], experts, capacity, gates_b, returned)
    slots_b = lax.optimization_barrier((slots_b, arrived))[0]
    slots_f = dispatch(me, routes_f, arrived, experts, capacity)

    z_start("b", slots_b, 0)
    z_start("f", slots_f, 0)
    z_start("b", slots_b, 4)
    x_start(0)
    z_start("b", slots_b, 1)
    x_join(0, [0])
    meet(("b", 4), ("b", 1), ("x", 0), ("fx", 0))
    x_start(1)
    z_start("b", slots_b, 5)
    x_start(4)
    z_start("b", slots_b, 2)
    meet(("b", 5), ("b", 2), ("x", 1), ("x", 4))
    x_start(2)
    z_start("b", slots_b, 6)
    x_start(5)
    z_start("b", slots_b, 3)
    meet(("b", 6), ("b", 3), ("x", 2), ("x", 5))
    x_start(3)
    z_start("b", slots_b, 7)
    x_start(6)
    z_start("f", slots_f, 1)
    meet(("b", 7), ("f", 1), ("x", 3), ("x", 6))
    x_start(7)
    z_start("f", slots_f, 4)
    z_start("f", slots_f, 2)
    back_own, kept_own = backward_half(
        [a for i in range(8) for a in held["b", i]], *weights, split
    )
    meet(("x", 7), ("f", 4), ("f", 2))
    met.append(kept_own[1])
    x_join(1, [1, 2, 4])
    z_start("f", slots_f, 5)
    z_start("f", slots_f, 3)
    back_other, kept_other = backward_half(
        [a for i in range(8) for a in held["x", i]], *weights, split
    )
    meet(("f", 5), ("f", 3), ("fx", 1))
    met.append(kept_other[1])
    part_start("rx", back_other, 2)
    z_start("f", slots_f, 6)
    part_start("rx", back_other, 3)
    z_start("f", slots_f, 7)
    meet(("rx", 2), ("f", 6), ("f", 7), ("rx", 3))
    x_join(2, [3, 5, 6, 7])
    give_back("r", back_own, 4)
    give_back("r", back_own, 5)
    out_own = forward_half([a for i in range(8) for a in held["f", i]], *weights, split)
    meet(("r", 4), ("r", 5), ("fx", 2))
    part_start("rx", back_other, 1)
    give_back("r", back_own, 6)
    give_back("r", back_own, 7)
    other_rows = held["fx", 0] + held["fx", 1] + held["fx", 2]
    out_other = forward_half(other_rows, *weights, split, [0, 1, 2, 4, 3, 5, 6, 7])
    part_start("ox", out_other, 2)
    meet(("rx", 1), ("r", 6), ("r", 7), ("ox", 2))
    part_start("ox", out_other, 3)
    give_back("o", out_own, 4)
    part_start("ox", out_other, 1)
    give_back("o", out_own, 5)
    give_back("r", back_own, 2)
    give_back("r", back_own, 3)
    meet(("o", 4), ("o", 5), ("ox", 3), ("ox", 1), ("r", 2), ("r", 3))
    give_back("o", out_own, 6)
    give_back("o", out_own, 7)
    both_start(1)
    give_back("o", out_own, 2)
    meet(("bx", 1), ("o", 2))
    both_start(0)
    give_both(1)
    give_back("o", out_own, 3)
    give_both(0)

    outer = (((0,), (0,)), ((), ()))

    def weight_term(a, b, others):
        terms = []
        for kept in (kept_own, kept_other):
            left = lax.optimization_barrier((kept[a], *others))[0]
            terms.append(lax.dot_general(left, kept[b], outer, preferred_element_type=jnp.float32))
        return (terms[0] + terms[1]).astype(jnp.bfloat16)

    grad_gate = weight_term(3, 1, rounds[6])
    grad_up = weight_term(3, 2, rounds[7])
    grad_down = weight_term(0, 4, rounds[8])

    back = [a for i in range(8) for a in held["r", i]]
    out = [a for i in range(8) for a in held["o", i]]
    grad_in = combine(me, routes_b, back, experts, capacity)
    layer_out = combine(me, routes_f, out, experts, capacity, gates_f)
    return (
        layer_out[None],
        grad_in[None],
        grad_gate[None, None],
        grad_up[None, None],
        grad_down[None, None],
    )


def solution(mesh):
    rows = P("section", "expert", None)
    weights = P("section", "expert", None, None)
    return jax.shard_map(
        per_device,
        mesh=mesh,
        in_specs=(rows,) * 7 + (weights,) * 3,
        out_specs=(rows, rows, weights, weights, weights),
        check_vma=False,
    )
```

```python
import functools

import jax
import jax.numpy as jnp
from jax import lax
from jax.experimental import pallas as pl
from jax.experimental.pallas import tpu as pltpu
from jax.sharding import PartitionSpec as P

VMEM_LIMIT = 48 << 20


def whole(n):
    return [pl.BlockSpec(memory_space=pltpu.VMEM)] * n


def params():
    return pltpu.CompilerParams(vmem_limit_bytes=VMEM_LIMIT)


def placement(me, routes, experts, capacity):
    tokens = routes.shape[1]
    rel = lax.bitwise_xor(routes, me)
    expert_row = lax.broadcasted_iota(jnp.int32, (experts, tokens), 0)
    first = rel[0:1, :] == expert_row
    second = rel[1:2, :] == expert_row
    hits = (first | second).astype(jnp.bfloat16)
    before = lax.broadcasted_iota(jnp.int32, (tokens, tokens), 0) < lax.broadcasted_iota(
        jnp.int32, (tokens, tokens), 1
    )
    earlier = jnp.dot(hits, before.astype(jnp.bfloat16), preferred_element_type=jnp.float32)
    slot0 = jnp.sum(jnp.where(first, earlier, 0.0), axis=0, keepdims=True).astype(jnp.int32)
    slot1 = jnp.sum(jnp.where(second, earlier, 0.0), axis=0, keepdims=True).astype(jnp.int32)
    place = lax.broadcasted_iota(jnp.int32, (experts * capacity, tokens), 0)
    at0 = place == rel[0:1, :] * capacity + slot0
    at1 = place == rel[1:2, :] * capacity + slot1
    return at0, at1


def as_bf16(mask):
    return mask.astype(jnp.float32).astype(jnp.bfloat16)


def dispatch_kernel(experts, capacity, me_ref, routes_ref, *refs):
    out_refs = refs[-experts:]
    at0, at1 = placement(me_ref[0], routes_ref[...], experts, capacity)
    table = as_bf16(at0 | at1)
    picked = jnp.dot(table, refs[0][...], preferred_element_type=jnp.float32).astype(jnp.bfloat16)
    for i, out in enumerate(out_refs):
        out[0:capacity, :] = picked[i * capacity : (i + 1) * capacity, :]
    if len(refs) == experts + 3:
        gates_ref, upstream_ref = refs[1:3]
        gate = jnp.where(at0, gates_ref[0:1, :], 0.0) + jnp.where(at1, gates_ref[1:2, :], 0.0)
        scaled = jnp.dot(table, upstream_ref[...], preferred_element_type=jnp.float32)
        scaled = (scaled * jnp.sum(gate, axis=1, keepdims=True)).astype(jnp.bfloat16)
        for i, out in enumerate(out_refs):
            out[capacity:, :] = scaled[i * capacity : (i + 1) * capacity, :]


def dispatch(me, routes, values, experts, capacity, gates=None, upstream=None):
    width = values.shape[1]
    many = 1 if gates is None else 2
    operands = (me, routes, values) + (() if gates is None else (gates, upstream))
    return pl.pallas_call(
        functools.partial(dispatch_kernel, experts, capacity),
        out_shape=[jax.ShapeDtypeStruct((many * capacity, width), jnp.bfloat16)] * experts,
        in_specs=[pl.BlockSpec(memory_space=pltpu.SMEM)] + whole(len(operands) - 1),
        out_specs=whole(experts),
        compiler_params=params(),
        cost_estimate=pl.CostEstimate(
            flops=2 * many * experts * capacity * values.size,
            bytes_accessed=2 * many * (values.size + experts * capacity * width),
            transcendentals=0,
        ),
        name="dispatch",
    )(*operands)


def combine_kernel(experts, capacity, scaled, me_ref, routes_ref, *refs):
    if scaled:
        gates_ref, *refs = refs
    *in_refs, out_ref, rows = refs
    for i, ref in enumerate(in_refs):
        rows[i * capacity : (i + 1) * capacity, :] = ref[...]
    at0, at1 = placement(me_ref[0], routes_ref[...], experts, capacity)
    outer = (((0,), (0,)), ((), ()))

    def pick(table):
        return lax.dot_general(
            table, rows[...], outer, preferred_element_type=jnp.float32
        )

    if scaled:
        gate = jnp.where(at0, gates_ref[0:1, :], 0.0) + jnp.where(at1, gates_ref[1:2, :], 0.0)
        high = gate.astype(jnp.bfloat16)
        low = (gate - high.astype(jnp.float32)).astype(jnp.bfloat16)
        out_ref[...] = (pick(high) + pick(low)).astype(jnp.bfloat16)
    else:
        out_ref[...] = pick(as_bf16(at0 | at1)).astype(jnp.bfloat16)


def combine(me, routes, pieces, experts, capacity, gates=None):
    width = pieces[0].shape[1]
    tokens = routes.shape[1]
    operands = (me, routes) + (() if gates is None else (gates,)) + tuple(pieces)
    return pl.pallas_call(
        functools.partial(combine_kernel, experts, capacity, gates is not None),
        out_shape=jax.ShapeDtypeStruct((tokens, width), jnp.bfloat16),
        in_specs=[pl.BlockSpec(memory_space=pltpu.SMEM)] + whole(len(operands) - 1),
        out_specs=pl.BlockSpec(memory_space=pltpu.VMEM),
        scratch_shapes=[pltpu.VMEM((experts * capacity, width), jnp.bfloat16)],
        compiler_params=params(),
        cost_estimate=pl.CostEstimate(
            flops=2 * tokens * experts * capacity * width,
            bytes_accessed=2 * (tokens * width + experts * capacity * width),
            transcendentals=0,
        ),
        name="combine",
    )(*operands)


def put(out_refs, values, order):
    step, at, places = values.shape[0] // len(order), 0, {}
    for out in out_refs:
        for row in range(0, out.shape[0], step):
            places[at] = (out, row)
            at += 1
    for n, i in enumerate(order):
        out, row = places[i]
        out[row : row + step, :] = values[n * step : (n + 1) * step, :]


def forward_kernel(pieces, outs, order, *refs):
    in_refs = refs[:pieces]
    gate_ref, up_ref, down_ref = refs[pieces : pieces + 3]
    out_refs = refs[pieces + 3 : pieces + 3 + outs]
    rows = refs[-1]
    at = 0
    for ref in in_refs:
        rows[at : at + ref.shape[0], :] = ref[...]
        at += ref.shape[0]
    gate_act = jnp.dot(rows[...], gate_ref[...], preferred_element_type=jnp.float32)
    up_act = jnp.dot(rows[...], up_ref[...], preferred_element_type=jnp.float32)
    hidden = (gate_act * jax.nn.sigmoid(gate_act) * up_act).astype(jnp.bfloat16)
    part = jnp.dot(hidden, down_ref[...], preferred_element_type=jnp.float32).astype(jnp.bfloat16)
    put(out_refs, part, order)


def forward_half(pieces, gate, up, down, outs, order=None):
    n = len(pieces)
    total = sum(piece.shape[0] for piece in pieces)
    width, hidden = gate.shape
    return pl.pallas_call(
        functools.partial(forward_kernel, n, len(outs), order or range(8)),
        out_shape=[jax.ShapeDtypeStruct((rows, width), jnp.bfloat16) for rows in outs],
        in_specs=whole(n + 3),
        out_specs=whole(len(outs)),
        scratch_shapes=[pltpu.VMEM((total, width), jnp.bfloat16)],
        compiler_params=params(),
        cost_estimate=pl.CostEstimate(
            flops=6 * total * width * hidden,
            bytes_accessed=4 * total * width + 6 * width * hidden,
            transcendentals=total * hidden,
        ),
        name="forward_half",
    )(*pieces, gate, up, down)


def backward_kernel(pieces, outs, *refs):
    in_refs = refs[:pieces]
    gate_ref, up_ref, down_ref = refs[pieces : pieces + 3]
    out_refs = refs[pieces + 3 : pieces + 3 + outs]
    hidden_ref, d_gate_ref, d_up_ref, rows, upstream = refs[pieces + 3 + outs :]
    half = in_refs[0].shape[0] // 2
    for i, ref in enumerate(in_refs):
        rows[i * half : (i + 1) * half, :] = ref[0:half, :]
        upstream[i * half : (i + 1) * half, :] = ref[half:, :]
    inner = (((1,), (1,)), ((), ()))
    gate_act = jnp.dot(rows[...], gate_ref[...], preferred_element_type=jnp.float32)
    up_act = jnp.dot(rows[...], up_ref[...], preferred_element_type=jnp.float32)
    d_hidden = lax.dot_general(
        upstream[...], down_ref[...], inner, preferred_element_type=jnp.float32
    )
    sigma = jax.nn.sigmoid(gate_act)
    swish = gate_act * sigma
    hidden_ref[...] = (swish * up_act).astype(jnp.bfloat16)
    d_gate = (d_hidden * up_act * sigma * (1.0 + gate_act * (1.0 - sigma))).astype(jnp.bfloat16)
    d_up = (d_hidden * swish).astype(jnp.bfloat16)
    d_gate_ref[...] = d_gate
    d_up_ref[...] = d_up
    back = lax.dot_general(d_gate, gate_ref[...], inner, preferred_element_type=jnp.float32)
    back = back + lax.dot_general(d_up, up_ref[...], inner, preferred_element_type=jnp.float32)
    back = back.astype(jnp.bfloat16)
    put(out_refs, back, range(8))


def backward_half(pieces, gate, up, down, outs):
    n = len(pieces)
    total = sum(piece.shape[0] for piece in pieces) // 2
    width, hidden = gate.shape
    small = jax.ShapeDtypeStruct((total, hidden), jnp.bfloat16)
    large = jax.ShapeDtypeStruct((total, width), jnp.bfloat16)
    out = pl.pallas_call(
        functools.partial(backward_kernel, n, len(outs)),
        out_shape=[jax.ShapeDtypeStruct((rows, width), jnp.bfloat16) for rows in outs]
        + [small] * 3
        + [large] * 2,
        in_specs=whole(n + 3),
        out_specs=whole(len(outs) + 5),
        compiler_params=params(),
        cost_estimate=pl.CostEstimate(
            flops=10 * total * width * hidden,
            bytes_accessed=10 * total * width + 6 * width * hidden,
            transcendentals=total * hidden,
        ),
        name="backward_half",
    )(*pieces, gate, up, down)
    return out[: len(outs)], out[len(outs) :]


def add_pair(a, b):
    return (a.astype(jnp.float32) + b.astype(jnp.float32)).astype(jnp.bfloat16)


def per_device(
    sent_forward,
    grad_sent,
    saved_inputs,
    routes_forward,
    gates_forward,
    routes_backward,
    gates_backward,
    w_gate,
    w_up,
    w_down,
):
    devices = lax.axis_size("expert")
    experts = devices // 2
    sections = lax.axis_size("section")
    tokens = sent_forward.shape[1]
    chosen = routes_forward.shape[2]
    capacity = 3 * tokens * chosen // (2 * experts)
    me = (lax.axis_index("expert") // 2).astype(jnp.int32).reshape(1)

    def along(array, by):
        return lax.ppermute(array, "section", [(i, (i + by) % sections) for i in range(sections)])

    def to_xor(array, mask):
        return lax.ppermute(array, "expert", [(i, i ^ mask) for i in range(devices)])

    routes_f, gates_f = routes_forward[0].T, gates_forward[0].T
    routes_b, gates_b = routes_backward[0].T, gates_backward[0].T
    weights = w_gate[0, 0], w_up[0, 0], w_down[0, 0]
    span = experts // 8
    group = [list(range(i * span, (i + 1) * span)) for i in range(8)]
    lump = span * capacity
    split = [lump, lump, 2 * lump, 2 * lump, 2 * lump]

    held, met, rounds = {}, [], []

    def after_met(array):
        return lax.optimization_barrier((array, *met))[0] if met else array

    def start(name, arrays, masks):
        held[name] = [
            to_xor(after_met(a), m) if m else a for a, m in zip(arrays, masks, strict=True)
        ]

    def meet(*names):
        met[:] = [a for name in names for a in held[name]]
        rounds.append(list(met))

    def z_start(kind, slots, i):
        start((kind, i), [slots[d] for d in group[i]], [2 * d for d in group[i]])

    def x_start(i):
        start(("x", i), held["b", i], [1] * span)

    def x_join(q, members):
        rows = [a for i in members for a in held["f", i]]
        start(("fx", q), [jnp.concatenate(rows) if len(rows) > 1 else rows[0]], [1])

    def part_start(kind, parts, q):
        start((kind, q), [parts[q + 1]], [1])

    def both_start(i):
        start(("bx", i), [jnp.concatenate([back_other[i], out_other[i]])], [1])

    def give_back(kind, own, i):
        q, first = i // 2, (i % 2) * span
        both = []
        for n in range(span):
            rows = slice((first + n) * capacity, (first + n + 1) * capacity)
            both.append(add_pair(own[q + 1][rows], held[kind + "x", q][0][rows]))
        start((kind, i), both, [2 * d for d in group[i]])

    def give_both(i):
        both = []
        for n in range(span):
            own_rows = slice(n * capacity, (n + 1) * capacity)
            met_rows = slice(lump + n * capacity, lump + (n + 1) * capacity)
            pair = [
                add_pair(back_own[i][own_rows], held["bx", i][0][own_rows]),
                add_pair(out_own[i][own_rows], held["bx", i][0][met_rows]),
            ]
            both.append(jnp.concatenate(pair))
        start(("both", i), both, [2 * d for d in group[i]])
        held["r", i] = [a[:capacity] for a in held["both", i]]
        held["o", i] = [a[capacity:] for a in held["both", i]]

    returned = along(grad_sent, -1)[0]
    arrived = along(sent_forward, 1)[0]
    slots_b = dispatch(me, routes_b, saved_inputs[0], experts, capacity, gates_b, returned)
    slots_b = lax.optimization_barrier((slots_b, arrived))[0]
    slots_f = dispatch(me, routes_f, arrived, experts, capacity)

    z_start("b", slots_b, 0)
    z_start("f", slots_f, 0)
    z_start("b", slots_b, 4)
    x_start(0)
    z_start("b", slots_b, 1)
    x_join(0, [0])
    meet(("b", 4),)
    z_start("b", slots_b, 5)
    meet(("b", 4), ("b", 1), ("x", 0), ("fx", 0))
    x_start(1)
    x_start(4)
    z_start("b", slots_b, 2)
    meet(("b", 5),)
    z_start("b", slots_b, 6)
    meet(("b", 5), ("b", 2), ("x", 1), ("x", 4))
    x_start(2)
    x_start(5)
    z_start("b", slots_b, 3)
    meet(("b", 6),)
    z_start("b", slots_b, 7)
    meet(("b", 6), ("b", 3), ("x", 2), ("x", 5))
    x_start(3)
    x_start(6)
    z_start("f", slots_f, 1)
    meet(("b", 7), ("f", 1), ("x", 3), ("x", 6))
    x_start(7)
    z_start("f", slots_f, 4)
    z_start("f", slots_f, 2)
    back_own, kept_own = backward_half(
        [a for i in range(8) for a in held["b", i]], *weights, split
    )
    meet(("x", 7), ("f", 4), ("f", 2))
    met.append(kept_own[1])
    x_join(1, [1, 2, 4])
    z_start("f", slots_f, 5)
    z_start("f", slots_f, 3)
    back_other, kept_other = backward_half(
        [a for i in range(8) for a in held["x", i]], *weights, split
    )
    meet(("f", 5), ("f", 3), ("fx", 1))
    met.append(kept_other[1])
    part_start("rx", back_other, 2)
    z_start("f", slots_f, 6)
    part_start("rx", back_other, 3)
    z_start("f", slots_f, 7)
    meet(("rx", 2), ("f", 6), ("f", 7), ("rx", 3))
    x_join(2, [3, 5, 6, 7])
    give_back("r", back_own, 4)
    give_back("r", back_own, 5)
    out_own = forward_half([a for i in range(8) for a in held["f", i]], *weights, split)
    meet(("r", 4), ("r", 5), ("fx", 2))
    part_start("rx", back_other, 1)
    give_back("r", back_own, 6)
    give_back("r", back_own, 7)
    other_rows = held["fx", 0] + held["fx", 1] + held["fx", 2]
    out_other = forward_half(other_rows, *weights, split, [0, 1, 2, 4, 3, 5, 6, 7])
    part_start("ox", out_other, 2)
    meet(("rx", 1), ("r", 6), ("r", 7), ("ox", 2))
    part_start("ox", out_other, 3)
    give_back("o", out_own, 4)
    both_start(1)
    give_back("o", out_own, 5)
    give_back("r", back_own, 3)
    meet(("o", 4), ("o", 5))
    give_back("o", out_own, 6)
    meet(("o", 4), ("o", 5), ("ox", 3), ("bx", 1), ("r", 3))
    part_start("ox", out_other, 1)
    give_both(1)
    give_back("r", back_own, 2)
    meet(("o", 6),)
    give_back("o", out_own, 7)
    meet(("o", 6), ("ox", 1), ("both", 1), ("r", 2))
    both_start(0)
    give_back("o", out_own, 2)
    give_back("o", out_own, 3)
    give_both(0)

    outer = (((0,), (0,)), ((), ()))

    def weight_term(a, b, others):
        terms = []
        for kept in (kept_own, kept_other):
            left = lax.optimization_barrier((kept[a], *others))[0]
            terms.append(lax.dot_general(left, kept[b], outer, preferred_element_type=jnp.float32))
        return (terms[0] + terms[1]).astype(jnp.bfloat16)

    grad_gate = weight_term(3, 1, rounds[9])
    grad_up = weight_term(3, 2, rounds[10])
    grad_down = weight_term(0, 4, rounds[11])

    back = [a for i in range(8) for a in held["r", i]]
    out = [a for i in range(8) for a in held["o", i]]
    grad_in = combine(me, routes_b, back, experts, capacity)
    layer_out = combine(me, routes_f, out, experts, capacity, gates_f)
    return (
        layer_out[None],
        grad_in[None],
        grad_gate[None, None],
        grad_up[None, None],
        grad_down[None, None],
    )


def solution(mesh):
    rows = P("section", "expert", None)
    weights = P("section", "expert", None, None)
    return jax.shard_map(
        per_device,
        mesh=mesh,
        in_specs=(rows,) * 7 + (weights,) * 3,
        out_specs=(rows, rows, weights, weights, weights),
        check_vma=False,
    )
```

```python
import functools

import jax
import jax.numpy as jnp
from jax import lax
from jax.experimental import pallas as pl
from jax.experimental.pallas import tpu as pltpu
from jax.sharding import PartitionSpec as P

VMEM_LIMIT = 48 << 20


def whole(n):
    return [pl.BlockSpec(memory_space=pltpu.VMEM)] * n


def params():
    return pltpu.CompilerParams(vmem_limit_bytes=VMEM_LIMIT)


def placement(me, routes, experts, capacity):
    tokens = routes.shape[1]
    rel = lax.bitwise_xor(routes, me)
    expert_row = lax.broadcasted_iota(jnp.int32, (experts, tokens), 0)
    first = rel[0:1, :] == expert_row
    second = rel[1:2, :] == expert_row
    hits = (first | second).astype(jnp.bfloat16)
    before = lax.broadcasted_iota(jnp.int32, (tokens, tokens), 0) < lax.broadcasted_iota(
        jnp.int32, (tokens, tokens), 1
    )
    earlier = jnp.dot(hits, before.astype(jnp.bfloat16), preferred_element_type=jnp.float32)
    slot0 = jnp.sum(jnp.where(first, earlier, 0.0), axis=0, keepdims=True).astype(jnp.int32)
    slot1 = jnp.sum(jnp.where(second, earlier, 0.0), axis=0, keepdims=True).astype(jnp.int32)
    place = lax.broadcasted_iota(jnp.int32, (experts * capacity, tokens), 0)
    at0 = place == rel[0:1, :] * capacity + slot0
    at1 = place == rel[1:2, :] * capacity + slot1
    return at0, at1


def as_bf16(mask):
    return mask.astype(jnp.float32).astype(jnp.bfloat16)


def dispatch_kernel(experts, capacity, me_ref, routes_ref, *refs):
    out_refs = refs[-experts:]
    at0, at1 = placement(me_ref[0], routes_ref[...], experts, capacity)
    table = as_bf16(at0 | at1)
    picked = jnp.dot(table, refs[0][...], preferred_element_type=jnp.float32).astype(jnp.bfloat16)
    for i, out in enumerate(out_refs):
        out[0:capacity, :] = picked[i * capacity : (i + 1) * capacity, :]
    if len(refs) == experts + 3:
        gates_ref, upstream_ref = refs[1:3]
        gate = jnp.where(at0, gates_ref[0:1, :], 0.0) + jnp.where(at1, gates_ref[1:2, :], 0.0)
        scaled = jnp.dot(table, upstream_ref[...], preferred_element_type=jnp.float32)
        scaled = (scaled * jnp.sum(gate, axis=1, keepdims=True)).astype(jnp.bfloat16)
        for i, out in enumerate(out_refs):
            out[capacity:, :] = scaled[i * capacity : (i + 1) * capacity, :]


def dispatch(me, routes, values, experts, capacity, gates=None, upstream=None):
    width = values.shape[1]
    many = 1 if gates is None else 2
    operands = (me, routes, values) + (() if gates is None else (gates, upstream))
    return pl.pallas_call(
        functools.partial(dispatch_kernel, experts, capacity),
        out_shape=[jax.ShapeDtypeStruct((many * capacity, width), jnp.bfloat16)] * experts,
        in_specs=[pl.BlockSpec(memory_space=pltpu.SMEM)] + whole(len(operands) - 1),
        out_specs=whole(experts),
        compiler_params=params(),
        cost_estimate=pl.CostEstimate(
            flops=2 * many * experts * capacity * values.size,
            bytes_accessed=2 * many * (values.size + experts * capacity * width),
            transcendentals=0,
        ),
        name="dispatch",
    )(*operands)


def combine_kernel(experts, capacity, scaled, me_ref, routes_ref, *refs):
    if scaled:
        gates_ref, *refs = refs
    *in_refs, out_ref, rows = refs
    for i, ref in enumerate(in_refs):
        rows[i * capacity : (i + 1) * capacity, :] = ref[...]
    at0, at1 = placement(me_ref[0], routes_ref[...], experts, capacity)
    outer = (((0,), (0,)), ((), ()))

    def pick(table):
        return lax.dot_general(
            table, rows[...], outer, preferred_element_type=jnp.float32
        )

    if scaled:
        gate = jnp.where(at0, gates_ref[0:1, :], 0.0) + jnp.where(at1, gates_ref[1:2, :], 0.0)
        high = gate.astype(jnp.bfloat16)
        low = (gate - high.astype(jnp.float32)).astype(jnp.bfloat16)
        out_ref[...] = (pick(high) + pick(low)).astype(jnp.bfloat16)
    else:
        out_ref[...] = pick(as_bf16(at0 | at1)).astype(jnp.bfloat16)


def combine(me, routes, pieces, experts, capacity, gates=None):
    width = pieces[0].shape[1]
    tokens = routes.shape[1]
    operands = (me, routes) + (() if gates is None else (gates,)) + tuple(pieces)
    return pl.pallas_call(
        functools.partial(combine_kernel, experts, capacity, gates is not None),
        out_shape=jax.ShapeDtypeStruct((tokens, width), jnp.bfloat16),
        in_specs=[pl.BlockSpec(memory_space=pltpu.SMEM)] + whole(len(operands) - 1),
        out_specs=pl.BlockSpec(memory_space=pltpu.VMEM),
        scratch_shapes=[pltpu.VMEM((experts * capacity, width), jnp.bfloat16)],
        compiler_params=params(),
        cost_estimate=pl.CostEstimate(
            flops=2 * tokens * experts * capacity * width,
            bytes_accessed=2 * (tokens * width + experts * capacity * width),
            transcendentals=0,
        ),
        name="combine",
    )(*operands)


def put(out_refs, values, order):
    step, at, places = values.shape[0] // len(order), 0, {}
    for out in out_refs:
        for row in range(0, out.shape[0], step):
            places[at] = (out, row)
            at += 1
    for n, i in enumerate(order):
        out, row = places[i]
        out[row : row + step, :] = values[n * step : (n + 1) * step, :]


def forward_kernel(pieces, outs, order, *refs):
    in_refs = refs[:pieces]
    gate_ref, up_ref, down_ref = refs[pieces : pieces + 3]
    out_refs = refs[pieces + 3 : pieces + 3 + outs]
    rows = refs[-1]
    at = 0
    for ref in in_refs:
        rows[at : at + ref.shape[0], :] = ref[...]
        at += ref.shape[0]
    gate_act = jnp.dot(rows[...], gate_ref[...], preferred_element_type=jnp.float32)
    up_act = jnp.dot(rows[...], up_ref[...], preferred_element_type=jnp.float32)
    hidden = (gate_act * jax.nn.sigmoid(gate_act) * up_act).astype(jnp.bfloat16)
    part = jnp.dot(hidden, down_ref[...], preferred_element_type=jnp.float32).astype(jnp.bfloat16)
    put(out_refs, part, order)


def forward_half(pieces, gate, up, down, outs, order=None):
    n = len(pieces)
    total = sum(piece.shape[0] for piece in pieces)
    width, hidden = gate.shape
    return pl.pallas_call(
        functools.partial(forward_kernel, n, len(outs), order or range(8)),
        out_shape=[jax.ShapeDtypeStruct((rows, width), jnp.bfloat16) for rows in outs],
        in_specs=whole(n + 3),
        out_specs=whole(len(outs)),
        scratch_shapes=[pltpu.VMEM((total, width), jnp.bfloat16)],
        compiler_params=params(),
        cost_estimate=pl.CostEstimate(
            flops=6 * total * width * hidden,
            bytes_accessed=4 * total * width + 6 * width * hidden,
            transcendentals=total * hidden,
        ),
        name="forward_half",
    )(*pieces, gate, up, down)


def backward_kernel(pieces, outs, *refs):
    in_refs = refs[:pieces]
    gate_ref, up_ref, down_ref = refs[pieces : pieces + 3]
    out_refs = refs[pieces + 3 : pieces + 3 + outs]
    hidden_ref, d_gate_ref, d_up_ref, rows, upstream = refs[pieces + 3 + outs :]
    half = in_refs[0].shape[0] // 2
    for i, ref in enumerate(in_refs):
        rows[i * half : (i + 1) * half, :] = ref[0:half, :]
        upstream[i * half : (i + 1) * half, :] = ref[half:, :]
    inner = (((1,), (1,)), ((), ()))
    gate_act = jnp.dot(rows[...], gate_ref[...], preferred_element_type=jnp.float32)
    up_act = jnp.dot(rows[...], up_ref[...], preferred_element_type=jnp.float32)
    d_hidden = lax.dot_general(
        upstream[...], down_ref[...], inner, preferred_element_type=jnp.float32
    )
    sigma = jax.nn.sigmoid(gate_act)
    swish = gate_act * sigma
    hidden_ref[...] = (swish * up_act).astype(jnp.bfloat16)
    d_gate = (d_hidden * up_act * sigma * (1.0 + gate_act * (1.0 - sigma))).astype(jnp.bfloat16)
    d_up = (d_hidden * swish).astype(jnp.bfloat16)
    d_gate_ref[...] = d_gate
    d_up_ref[...] = d_up
    back = lax.dot_general(d_gate, gate_ref[...], inner, preferred_element_type=jnp.float32)
    back = back + lax.dot_general(d_up, up_ref[...], inner, preferred_element_type=jnp.float32)
    back = back.astype(jnp.bfloat16)
    put(out_refs, back, range(8))


def backward_half(pieces, gate, up, down, outs):
    n = len(pieces)
    total = sum(piece.shape[0] for piece in pieces) // 2
    width, hidden = gate.shape
    small = jax.ShapeDtypeStruct((total, hidden), jnp.bfloat16)
    large = jax.ShapeDtypeStruct((total, width), jnp.bfloat16)
    out = pl.pallas_call(
        functools.partial(backward_kernel, n, len(outs)),
        out_shape=[jax.ShapeDtypeStruct((rows, width), jnp.bfloat16) for rows in outs]
        + [small] * 3
        + [large] * 2,
        in_specs=whole(n + 3),
        out_specs=whole(len(outs) + 5),
        compiler_params=params(),
        cost_estimate=pl.CostEstimate(
            flops=10 * total * width * hidden,
            bytes_accessed=10 * total * width + 6 * width * hidden,
            transcendentals=total * hidden,
        ),
        name="backward_half",
    )(*pieces, gate, up, down)
    return out[: len(outs)], out[len(outs) :]


def add_pair(a, b):
    return (a.astype(jnp.float32) + b.astype(jnp.float32)).astype(jnp.bfloat16)


def per_device(
    sent_forward,
    grad_sent,
    saved_inputs,
    routes_forward,
    gates_forward,
    routes_backward,
    gates_backward,
    w_gate,
    w_up,
    w_down,
):
    devices = lax.axis_size("expert")
    experts = devices // 2
    sections = lax.axis_size("section")
    tokens = sent_forward.shape[1]
    chosen = routes_forward.shape[2]
    capacity = 3 * tokens * chosen // (2 * experts)
    me = (lax.axis_index("expert") // 2).astype(jnp.int32).reshape(1)

    def along(array, by):
        return lax.ppermute(array, "section", [(i, (i + by) % sections) for i in range(sections)])

    def to_xor(array, mask):
        return lax.ppermute(array, "expert", [(i, i ^ mask) for i in range(devices)])

    routes_f, gates_f = routes_forward[0].T, gates_forward[0].T
    routes_b, gates_b = routes_backward[0].T, gates_backward[0].T
    weights = w_gate[0, 0], w_up[0, 0], w_down[0, 0]
    span = experts // 8
    group = [list(range(i * span, (i + 1) * span)) for i in range(8)]
    lump = span * capacity
    split = [lump, lump, 2 * lump, 2 * lump, 2 * lump]

    held, met, rounds = {}, [], []

    def after_met(array):
        return lax.optimization_barrier((array, *met))[0] if met else array

    def start(name, arrays, masks):
        held[name] = [
            to_xor(after_met(a), m) if m else a for a, m in zip(arrays, masks, strict=True)
        ]

    def meet(*names):
        met[:] = [a for name in names for a in held[name]]
        rounds.append(list(met))

    def z_start(kind, slots, i):
        start((kind, i), [slots[d] for d in group[i]], [2 * d for d in group[i]])

    def x_start(i):
        start(("x", i), held["b", i], [1] * span)

    def x_join(q, members):
        rows = [a for i in members for a in held["f", i]]
        start(("fx", q), [jnp.concatenate(rows) if len(rows) > 1 else rows[0]], [1])

    def part_start(kind, parts, q):
        start((kind, q), [parts[q + 1]], [1])

    def both_start(i):
        start(("bx", i), [jnp.concatenate([back_other[i], out_other[i]])], [1])

    def give_back(kind, own, i):
        q, first = i // 2, (i % 2) * span
        both = []
        for n in range(span):
            rows = slice((first + n) * capacity, (first + n + 1) * capacity)
            both.append(add_pair(own[q + 1][rows], held[kind + "x", q][0][rows]))
        start((kind, i), both, [2 * d for d in group[i]])

    def give_both(i):
        both = []
        for n in range(span):
            own_rows = slice(n * capacity, (n + 1) * capacity)
            met_rows = slice(lump + n * capacity, lump + (n + 1) * capacity)
            pair = [
                add_pair(back_own[i][own_rows], held["bx", i][0][own_rows]),
                add_pair(out_own[i][own_rows], held["bx", i][0][met_rows]),
            ]
            both.append(jnp.concatenate(pair))
        start(("both", i), both, [2 * d for d in group[i]])
        held["r", i] = [a[:capacity] for a in held["both", i]]
        held["o", i] = [a[capacity:] for a in held["both", i]]

    returned = along(grad_sent, -1)[0]
    arrived = along(sent_forward, 1)[0]
    slots_b = dispatch(me, routes_b, saved_inputs[0], experts, capacity, gates_b, returned)
    slots_b = lax.optimization_barrier((slots_b, arrived))[0]
    slots_f = dispatch(me, routes_f, arrived, experts, capacity)

    z_start("b", slots_b, 0)
    z_start("f", slots_f, 0)
    z_start("b", slots_b, 4)
    x_start(0)
    z_start("b", slots_b, 1)
    x_join(0, [0])
    meet(("b", 4),)
    z_start("b", slots_b, 5)
    meet(("b", 4), ("b", 1), ("x", 0), ("fx", 0))
    x_start(1)
    x_start(4)
    z_start("b", slots_b, 2)
    meet(("b", 5),)
    z_start("b", slots_b, 6)
    meet(("b", 5), ("b", 2), ("x", 1), ("x", 4))
    x_start(2)
    x_start(5)
    z_start("b", slots_b, 3)
    meet(("b", 6),)
    z_start("b", slots_b, 7)
    meet(("b", 6), ("b", 3), ("x", 2), ("x", 5))
    x_start(3)
    x_start(6)
    z_start("f", slots_f, 1)
    meet(("b", 7),)
    z_start("f", slots_f, 4)
    meet(("b", 7), ("f", 1), ("x", 3), ("x", 6))
    x_start(7)
    z_start("f", slots_f, 2)
    back_own, kept_own = backward_half(
        [a for i in range(8) for a in held["b", i]], *weights, split
    )
    meet(("x", 7), ("f", 4), ("f", 2))
    met.append(kept_own[1])
    x_join(1, [1, 2, 4])
    z_start("f", slots_f, 5)
    z_start("f", slots_f, 3)
    back_other, kept_other = backward_half(
        [a for i in range(8) for a in held["x", i]], *weights, split
    )
    meet(("f", 5), ("f", 3), ("fx", 1))
    met.append(kept_other[1])
    part_start("rx", back_other, 2)
    z_start("f", slots_f, 6)
    part_start("rx", back_other, 3)
    z_start("f", slots_f, 7)
    meet(("rx", 2), ("f", 6), ("f", 7), ("rx", 3))
    x_join(2, [3, 5, 6, 7])
    give_back("r", back_own, 4)
    give_back("r", back_own, 5)
    out_own = forward_half([a for i in range(8) for a in held["f", i]], *weights, split)
    meet(("r", 4), ("r", 5), ("fx", 2))
    part_start("rx", back_other, 1)
    give_back("r", back_own, 6)
    give_back("r", back_own, 7)
    other_rows = held["fx", 0] + held["fx", 1] + held["fx", 2]
    out_other = forward_half(other_rows, *weights, split, [0, 1, 2, 4, 3, 5, 6, 7])
    part_start("ox", out_other, 2)
    meet(("rx", 1), ("r", 6), ("r", 7), ("ox", 2))
    part_start("ox", out_other, 3)
    give_back("o", out_own, 4)
    both_start(1)
    give_back("o", out_own, 5)
    give_back("r", back_own, 3)
    meet(("o", 4), ("o", 5))
    give_back("o", out_own, 6)
    meet(("o", 4), ("o", 5), ("ox", 3), ("bx", 1), ("r", 3))
    part_start("ox", out_other, 1)
    give_both(1)
    give_back("r", back_own, 2)
    meet(("o", 6),)
    give_back("o", out_own, 7)
    meet(("o", 6), ("ox", 1), ("both", 1), ("r", 2))
    both_start(0)
    give_back("o", out_own, 2)
    give_back("o", out_own, 3)
    give_both(0)

    outer = (((0,), (0,)), ((), ()))

    def weight_term(a, b, others):
        terms = []
        for kept in (kept_own, kept_other):
            left = lax.optimization_barrier((kept[a], *others))[0]
            terms.append(lax.dot_general(left, kept[b], outer, preferred_element_type=jnp.float32))
        return (terms[0] + terms[1]).astype(jnp.bfloat16)

    grad_gate = weight_term(3, 1, rounds[10])
    grad_up = weight_term(3, 2, rounds[11])
    grad_down = weight_term(0, 4, rounds[12])

    back = [a for i in range(8) for a in held["r", i]]
    out = [a for i in range(8) for a in held["o", i]]
    grad_in = combine(me, routes_b, back, experts, capacity)
    layer_out = combine(me, routes_f, out, experts, capacity, gates_f)
    return (
        layer_out[None],
        grad_in[None],
        grad_gate[None, None],
        grad_up[None, None],
        grad_down[None, None],
    )


def solution(mesh):
    rows = P("section", "expert", None)
    weights = P("section", "expert", None, None)
    return jax.shard_map(
        per_device,
        mesh=mesh,
        in_specs=(rows,) * 7 + (weights,) * 3,
        out_specs=(rows, rows, weights, weights, weights),
        check_vma=False,
    )
```

```python
import functools

import jax
import jax.numpy as jnp
from jax import lax
from jax.experimental import pallas as pl
from jax.experimental.pallas import tpu as pltpu
from jax.sharding import PartitionSpec as P

VMEM_LIMIT = 48 << 20


def whole(n):
    return [pl.BlockSpec(memory_space=pltpu.VMEM)] * n


def params():
    return pltpu.CompilerParams(vmem_limit_bytes=VMEM_LIMIT)


def placement(me, routes, experts, capacity):
    tokens = routes.shape[1]
    rel = lax.bitwise_xor(routes, me)
    expert_row = lax.broadcasted_iota(jnp.int32, (experts, tokens), 0)
    first = rel[0:1, :] == expert_row
    second = rel[1:2, :] == expert_row
    hits = (first | second).astype(jnp.bfloat16)
    before = lax.broadcasted_iota(jnp.int32, (tokens, tokens), 0) < lax.broadcasted_iota(
        jnp.int32, (tokens, tokens), 1
    )
    earlier = jnp.dot(hits, before.astype(jnp.bfloat16), preferred_element_type=jnp.float32)
    slot0 = jnp.sum(jnp.where(first, earlier, 0.0), axis=0, keepdims=True).astype(jnp.int32)
    slot1 = jnp.sum(jnp.where(second, earlier, 0.0), axis=0, keepdims=True).astype(jnp.int32)
    place = lax.broadcasted_iota(jnp.int32, (experts * capacity, tokens), 0)
    at0 = place == rel[0:1, :] * capacity + slot0
    at1 = place == rel[1:2, :] * capacity + slot1
    return at0, at1


def as_bf16(mask):
    return mask.astype(jnp.float32).astype(jnp.bfloat16)


def dispatch_kernel(experts, capacity, me_ref, routes_ref, *refs):
    out_refs = refs[-experts:]
    at0, at1 = placement(me_ref[0], routes_ref[...], experts, capacity)
    table = as_bf16(at0 | at1)
    picked = jnp.dot(table, refs[0][...], preferred_element_type=jnp.float32).astype(jnp.bfloat16)
    for i, out in enumerate(out_refs):
        out[0:capacity, :] = picked[i * capacity : (i + 1) * capacity, :]
    if len(refs) == experts + 3:
        gates_ref, upstream_ref = refs[1:3]
        gate = jnp.where(at0, gates_ref[0:1, :], 0.0) + jnp.where(at1, gates_ref[1:2, :], 0.0)
        scaled = jnp.dot(table, upstream_ref[...], preferred_element_type=jnp.float32)
        scaled = (scaled * jnp.sum(gate, axis=1, keepdims=True)).astype(jnp.bfloat16)
        for i, out in enumerate(out_refs):
            out[capacity:, :] = scaled[i * capacity : (i + 1) * capacity, :]


def dispatch(me, routes, values, experts, capacity, gates=None, upstream=None):
    width = values.shape[1]
    many = 1 if gates is None else 2
    operands = (me, routes, values) + (() if gates is None else (gates, upstream))
    return pl.pallas_call(
        functools.partial(dispatch_kernel, experts, capacity),
        out_shape=[jax.ShapeDtypeStruct((many * capacity, width), jnp.bfloat16)] * experts,
        in_specs=[pl.BlockSpec(memory_space=pltpu.SMEM)] + whole(len(operands) - 1),
        out_specs=whole(experts),
        compiler_params=params(),
        cost_estimate=pl.CostEstimate(
            flops=2 * many * experts * capacity * values.size,
            bytes_accessed=2 * many * (values.size + experts * capacity * width),
            transcendentals=0,
        ),
        name="dispatch",
    )(*operands)


def combine_kernel(experts, capacity, scaled, me_ref, routes_ref, *refs):
    if scaled:
        gates_ref, *refs = refs
    *in_refs, out_ref, rows = refs
    for i, ref in enumerate(in_refs):
        rows[i * capacity : (i + 1) * capacity, :] = ref[...]
    at0, at1 = placement(me_ref[0], routes_ref[...], experts, capacity)
    outer = (((0,), (0,)), ((), ()))

    def pick(table):
        return lax.dot_general(
            table, rows[...], outer, preferred_element_type=jnp.float32
        )

    if scaled:
        gate = jnp.where(at0, gates_ref[0:1, :], 0.0) + jnp.where(at1, gates_ref[1:2, :], 0.0)
        high = gate.astype(jnp.bfloat16)
        low = (gate - high.astype(jnp.float32)).astype(jnp.bfloat16)
        out_ref[...] = (pick(high) + pick(low)).astype(jnp.bfloat16)
    else:
        out_ref[...] = pick(as_bf16(at0 | at1)).astype(jnp.bfloat16)


def combine(me, routes, pieces, experts, capacity, gates=None):
    width = pieces[0].shape[1]
    tokens = routes.shape[1]
    operands = (me, routes) + (() if gates is None else (gates,)) + tuple(pieces)
    return pl.pallas_call(
        functools.partial(combine_kernel, experts, capacity, gates is not None),
        out_shape=jax.ShapeDtypeStruct((tokens, width), jnp.bfloat16),
        in_specs=[pl.BlockSpec(memory_space=pltpu.SMEM)] + whole(len(operands) - 1),
        out_specs=pl.BlockSpec(memory_space=pltpu.VMEM),
        scratch_shapes=[pltpu.VMEM((experts * capacity, width), jnp.bfloat16)],
        compiler_params=params(),
        cost_estimate=pl.CostEstimate(
            flops=2 * tokens * experts * capacity * width,
            bytes_accessed=2 * (tokens * width + experts * capacity * width),
            transcendentals=0,
        ),
        name="combine",
    )(*operands)


def put(out_refs, values, order):
    step, at, places = values.shape[0] // len(order), 0, {}
    for out in out_refs:
        for row in range(0, out.shape[0], step):
            places[at] = (out, row)
            at += 1
    for n, i in enumerate(order):
        out, row = places[i]
        out[row : row + step, :] = values[n * step : (n + 1) * step, :]


def forward_kernel(pieces, outs, order, *refs):
    in_refs = refs[:pieces]
    gate_ref, up_ref, down_ref = refs[pieces : pieces + 3]
    out_refs = refs[pieces + 3 : pieces + 3 + outs]
    rows = refs[-1]
    at = 0
    for ref in in_refs:
        rows[at : at + ref.shape[0], :] = ref[...]
        at += ref.shape[0]
    gate_act = jnp.dot(rows[...], gate_ref[...], preferred_element_type=jnp.float32)
    up_act = jnp.dot(rows[...], up_ref[...], preferred_element_type=jnp.float32)
    hidden = (gate_act * jax.nn.sigmoid(gate_act) * up_act).astype(jnp.bfloat16)
    part = jnp.dot(hidden, down_ref[...], preferred_element_type=jnp.float32).astype(jnp.bfloat16)
    put(out_refs, part, order)


def forward_half(pieces, gate, up, down, outs, order=None):
    n = len(pieces)
    total = sum(piece.shape[0] for piece in pieces)
    width, hidden = gate.shape
    return pl.pallas_call(
        functools.partial(forward_kernel, n, len(outs), order or range(8)),
        out_shape=[jax.ShapeDtypeStruct((rows, width), jnp.bfloat16) for rows in outs],
        in_specs=whole(n + 3),
        out_specs=whole(len(outs)),
        scratch_shapes=[pltpu.VMEM((total, width), jnp.bfloat16)],
        compiler_params=params(),
        cost_estimate=pl.CostEstimate(
            flops=6 * total * width * hidden,
            bytes_accessed=4 * total * width + 6 * width * hidden,
            transcendentals=total * hidden,
        ),
        name="forward_half",
    )(*pieces, gate, up, down)


def backward_kernel(pieces, outs, *refs):
    in_refs = refs[:pieces]
    gate_ref, up_ref, down_ref = refs[pieces : pieces + 3]
    out_refs = refs[pieces + 3 : pieces + 3 + outs]
    hidden_ref, d_gate_ref, d_up_ref, rows, upstream = refs[pieces + 3 + outs :]
    half = in_refs[0].shape[0] // 2
    for i, ref in enumerate(in_refs):
        rows[i * half : (i + 1) * half, :] = ref[0:half, :]
        upstream[i * half : (i + 1) * half, :] = ref[half:, :]
    inner = (((1,), (1,)), ((), ()))
    gate_act = jnp.dot(rows[...], gate_ref[...], preferred_element_type=jnp.float32)
    up_act = jnp.dot(rows[...], up_ref[...], preferred_element_type=jnp.float32)
    d_hidden = lax.dot_general(
        upstream[...], down_ref[...], inner, preferred_element_type=jnp.float32
    )
    sigma = jax.nn.sigmoid(gate_act)
    swish = gate_act * sigma
    hidden_ref[...] = (swish * up_act).astype(jnp.bfloat16)
    d_gate = (d_hidden * up_act * sigma * (1.0 + gate_act * (1.0 - sigma))).astype(jnp.bfloat16)
    d_up = (d_hidden * swish).astype(jnp.bfloat16)
    d_gate_ref[...] = d_gate
    d_up_ref[...] = d_up
    back = lax.dot_general(d_gate, gate_ref[...], inner, preferred_element_type=jnp.float32)
    back = back + lax.dot_general(d_up, up_ref[...], inner, preferred_element_type=jnp.float32)
    back = back.astype(jnp.bfloat16)
    put(out_refs, back, range(8))


def backward_half(pieces, gate, up, down, outs):
    n = len(pieces)
    total = sum(piece.shape[0] for piece in pieces) // 2
    width, hidden = gate.shape
    small = jax.ShapeDtypeStruct((total, hidden), jnp.bfloat16)
    large = jax.ShapeDtypeStruct((total, width), jnp.bfloat16)
    out = pl.pallas_call(
        functools.partial(backward_kernel, n, len(outs)),
        out_shape=[jax.ShapeDtypeStruct((rows, width), jnp.bfloat16) for rows in outs]
        + [small] * 3
        + [large] * 2,
        in_specs=whole(n + 3),
        out_specs=whole(len(outs) + 5),
        compiler_params=params(),
        cost_estimate=pl.CostEstimate(
            flops=10 * total * width * hidden,
            bytes_accessed=10 * total * width + 6 * width * hidden,
            transcendentals=total * hidden,
        ),
        name="backward_half",
    )(*pieces, gate, up, down)
    return out[: len(outs)], out[len(outs) :]


def add_pair(a, b):
    return (a.astype(jnp.float32) + b.astype(jnp.float32)).astype(jnp.bfloat16)


def per_device(
    sent_forward,
    grad_sent,
    saved_inputs,
    routes_forward,
    gates_forward,
    routes_backward,
    gates_backward,
    w_gate,
    w_up,
    w_down,
):
    devices = lax.axis_size("expert")
    experts = devices // 2
    sections = lax.axis_size("section")
    tokens = sent_forward.shape[1]
    chosen = routes_forward.shape[2]
    capacity = 3 * tokens * chosen // (2 * experts)
    me = (lax.axis_index("expert") // 2).astype(jnp.int32).reshape(1)

    def along(array, by):
        return lax.ppermute(array, "section", [(i, (i + by) % sections) for i in range(sections)])

    def to_xor(array, mask):
        return lax.ppermute(array, "expert", [(i, i ^ mask) for i in range(devices)])

    routes_f, gates_f = routes_forward[0].T, gates_forward[0].T
    routes_b, gates_b = routes_backward[0].T, gates_backward[0].T
    weights = w_gate[0, 0], w_up[0, 0], w_down[0, 0]
    span = experts // 8
    group = [list(range(i * span, (i + 1) * span)) for i in range(8)]
    lump = span * capacity
    split = [lump, lump, 2 * lump, 2 * lump, 2 * lump]

    held, met, rounds = {}, [], []

    def after_met(array):
        return lax.optimization_barrier((array, *met))[0] if met else array

    def start(name, arrays, masks):
        held[name] = [
            to_xor(after_met(a), m) if m else a for a, m in zip(arrays, masks, strict=True)
        ]

    def meet(*names):
        met[:] = [a for name in names for a in held[name]]
        rounds.append(list(met))

    def z_start(kind, slots, i):
        start((kind, i), [slots[d] for d in group[i]], [2 * d for d in group[i]])

    def x_start(i):
        start(("x", i), held["b", i], [1] * span)

    def x_join(q, members):
        rows = [a for i in members for a in held["f", i]]
        start(("fx", q), [jnp.concatenate(rows) if len(rows) > 1 else rows[0]], [1])

    def part_start(kind, parts, q):
        start((kind, q), [parts[q + 1]], [1])

    def both_start(i):
        start(("bx", i), [jnp.concatenate([back_other[i], out_other[i]])], [1])

    def give_back(kind, own, i):
        q, first = i // 2, (i % 2) * span
        both = []
        for n in range(span):
            rows = slice((first + n) * capacity, (first + n + 1) * capacity)
            both.append(add_pair(own[q + 1][rows], held[kind + "x", q][0][rows]))
        start((kind, i), both, [2 * d for d in group[i]])

    def give_both(i):
        both = []
        for n in range(span):
            own_rows = slice(n * capacity, (n + 1) * capacity)
            met_rows = slice(lump + n * capacity, lump + (n + 1) * capacity)
            pair = [
                add_pair(back_own[i][own_rows], held["bx", i][0][own_rows]),
                add_pair(out_own[i][own_rows], held["bx", i][0][met_rows]),
            ]
            both.append(jnp.concatenate(pair))
        start(("both", i), both, [2 * d for d in group[i]])
        held["r", i] = [a[:capacity] for a in held["both", i]]
        held["o", i] = [a[capacity:] for a in held["both", i]]

    returned = along(grad_sent, -1)[0]
    arrived = along(sent_forward, 1)[0]
    slots_b = dispatch(me, routes_b, saved_inputs[0], experts, capacity, gates_b, returned)
    slots_b = lax.optimization_barrier((slots_b, arrived))[0]
    slots_f = dispatch(me, routes_f, arrived, experts, capacity)

    z_start("b", slots_b, 0)
    z_start("f", slots_f, 0)
    z_start("b", slots_b, 4)
    x_start(0)
    z_start("b", slots_b, 1)
    x_join(0, [0])
    meet(("b", 4),)
    z_start("b", slots_b, 5)
    meet(("b", 4), ("b", 1), ("x", 0), ("fx", 0))
    x_start(1)
    x_start(4)
    z_start("b", slots_b, 2)
    meet(("b", 5),)
    z_start("b", slots_b, 6)
    meet(("b", 5), ("b", 2), ("x", 1), ("x", 4))
    x_start(2)
    x_start(5)
    z_start("b", slots_b, 3)
    meet(("b", 6),)
    z_start("b", slots_b, 7)
    meet(("b", 6), ("b", 3), ("x", 2), ("x", 5))
    x_start(3)
    x_start(6)
    z_start("f", slots_f, 1)
    meet(("b", 7),)
    z_start("f", slots_f, 4)
    meet(("x", 3), ("x", 6))
    x_start(7)
    meet(("b", 7), ("f", 1), ("x", 3), ("x", 6))
    z_start("f", slots_f, 2)
    back_own, kept_own = backward_half(
        [a for i in range(8) for a in held["b", i]], *weights, split
    )
    meet(("x", 7), ("f", 4), ("f", 2))
    met.append(kept_own[1])
    x_join(1, [1, 2, 4])
    z_start("f", slots_f, 5)
    z_start("f", slots_f, 3)
    back_other, kept_other = backward_half(
        [a for i in range(8) for a in held["x", i]], *weights, split
    )
    meet(("f", 5), ("f", 3), ("fx", 1))
    met.append(kept_other[1])
    part_start("rx", back_other, 2)
    z_start("f", slots_f, 6)
    part_start("rx", back_other, 3)
    z_start("f", slots_f, 7)
    meet(("rx", 2), ("f", 6), ("f", 7), ("rx", 3))
    x_join(2, [3, 5, 6, 7])
    give_back("r", back_own, 4)
    give_back("r", back_own, 5)
    out_own = forward_half([a for i in range(8) for a in held["f", i]], *weights, split)
    meet(("r", 4), ("r", 5), ("fx", 2))
    part_start("rx", back_other, 1)
    give_back("r", back_own, 6)
    give_back("r", back_own, 7)
    other_rows = held["fx", 0] + held["fx", 1] + held["fx", 2]
    out_other = forward_half(other_rows, *weights, split, [0, 1, 2, 4, 3, 5, 6, 7])
    part_start("ox", out_other, 2)
    meet(("rx", 1), ("r", 6), ("r", 7), ("ox", 2))
    part_start("ox", out_other, 3)
    give_back("o", out_own, 4)
    both_start(1)
    give_back("o", out_own, 5)
    give_back("r", back_own, 3)
    meet(("o", 4), ("o", 5))
    give_back("o", out_own, 6)
    meet(("ox", 3), ("bx", 1))
    part_start("ox", out_other, 1)
    meet(("o", 4), ("o", 5), ("ox", 3), ("bx", 1), ("r", 3))
    give_both(1)
    give_back("r", back_own, 2)
    meet(("o", 6),)
    give_back("o", out_own, 7)
    meet(("o", 6), ("ox", 1), ("both", 1), ("r", 2))
    both_start(0)
    give_back("o", out_own, 2)
    give_back("o", out_own, 3)
    give_both(0)

    outer = (((0,), (0,)), ((), ()))

    def weight_term(a, b, others):
        terms = []
        for kept in (kept_own, kept_other):
            left = lax.optimization_barrier((kept[a], *others))[0]
            terms.append(lax.dot_general(left, kept[b], outer, preferred_element_type=jnp.float32))
        return (terms[0] + terms[1]).astype(jnp.bfloat16)

    grad_gate = weight_term(3, 1, rounds[11])
    grad_up = weight_term(3, 2, rounds[12])
    grad_down = weight_term(0, 4, rounds[13])

    back = [a for i in range(8) for a in held["r", i]]
    out = [a for i in range(8) for a in held["o", i]]
    grad_in = combine(me, routes_b, back, experts, capacity)
    layer_out = combine(me, routes_f, out, experts, capacity, gates_f)
    return (
        layer_out[None],
        grad_in[None],
        grad_gate[None, None],
        grad_up[None, None],
        grad_down[None, None],
    )


def solution(mesh):
    rows = P("section", "expert", None)
    weights = P("section", "expert", None, None)
    return jax.shard_map(
        per_device,
        mesh=mesh,
        in_specs=(rows,) * 7 + (weights,) * 3,
        out_specs=(rows, rows, weights, weights, weights),
        check_vma=False,
    )
```

```python
import functools

import jax
import jax.numpy as jnp
from jax import lax
from jax.experimental import pallas as pl
from jax.experimental.pallas import tpu as pltpu
from jax.sharding import PartitionSpec as P

VMEM_LIMIT = 48 << 20


def whole(n):
    return [pl.BlockSpec(memory_space=pltpu.VMEM)] * n


def params():
    return pltpu.CompilerParams(vmem_limit_bytes=VMEM_LIMIT)


def placement(me, routes, experts, capacity):
    tokens = routes.shape[1]
    rel = lax.bitwise_xor(routes, me)
    expert_row = lax.broadcasted_iota(jnp.int32, (experts, tokens), 0)
    first = rel[0:1, :] == expert_row
    second = rel[1:2, :] == expert_row
    hits = (first | second).astype(jnp.bfloat16)
    before = lax.broadcasted_iota(jnp.int32, (tokens, tokens), 0) < lax.broadcasted_iota(
        jnp.int32, (tokens, tokens), 1
    )
    earlier = jnp.dot(hits, before.astype(jnp.bfloat16), preferred_element_type=jnp.float32)
    slot0 = jnp.sum(jnp.where(first, earlier, 0.0), axis=0, keepdims=True).astype(jnp.int32)
    slot1 = jnp.sum(jnp.where(second, earlier, 0.0), axis=0, keepdims=True).astype(jnp.int32)
    place = lax.broadcasted_iota(jnp.int32, (experts * capacity, tokens), 0)
    at0 = place == rel[0:1, :] * capacity + slot0
    at1 = place == rel[1:2, :] * capacity + slot1
    return at0, at1


def as_bf16(mask):
    return mask.astype(jnp.float32).astype(jnp.bfloat16)


def dispatch_kernel(experts, capacity, me_ref, routes_ref, *refs):
    out_refs = refs[-experts:]
    at0, at1 = placement(me_ref[0], routes_ref[...], experts, capacity)
    table = as_bf16(at0 | at1)
    picked = jnp.dot(table, refs[0][...], preferred_element_type=jnp.float32).astype(jnp.bfloat16)
    for i, out in enumerate(out_refs):
        out[0:capacity, :] = picked[i * capacity : (i + 1) * capacity, :]
    if len(refs) == experts + 3:
        gates_ref, upstream_ref = refs[1:3]
        gate = jnp.where(at0, gates_ref[0:1, :], 0.0) + jnp.where(at1, gates_ref[1:2, :], 0.0)
        scaled = jnp.dot(table, upstream_ref[...], preferred_element_type=jnp.float32)
        scaled = (scaled * jnp.sum(gate, axis=1, keepdims=True)).astype(jnp.bfloat16)
        for i, out in enumerate(out_refs):
            out[capacity:, :] = scaled[i * capacity : (i + 1) * capacity, :]


def dispatch(me, routes, values, experts, capacity, gates=None, upstream=None):
    width = values.shape[1]
    many = 1 if gates is None else 2
    operands = (me, routes, values) + (() if gates is None else (gates, upstream))
    return pl.pallas_call(
        functools.partial(dispatch_kernel, experts, capacity),
        out_shape=[jax.ShapeDtypeStruct((many * capacity, width), jnp.bfloat16)] * experts,
        in_specs=[pl.BlockSpec(memory_space=pltpu.SMEM)] + whole(len(operands) - 1),
        out_specs=whole(experts),
        compiler_params=params(),
        cost_estimate=pl.CostEstimate(
            flops=2 * many * experts * capacity * values.size,
            bytes_accessed=2 * many * (values.size + experts * capacity * width),
            transcendentals=0,
        ),
        name="dispatch",
    )(*operands)


def combine_kernel(experts, capacity, scaled, me_ref, routes_ref, *refs):
    if scaled:
        gates_ref, *refs = refs
    *in_refs, out_ref, rows = refs
    for i, ref in enumerate(in_refs):
        rows[i * capacity : (i + 1) * capacity, :] = ref[...]
    at0, at1 = placement(me_ref[0], routes_ref[...], experts, capacity)
    outer = (((0,), (0,)), ((), ()))

    def pick(table):
        return lax.dot_general(
            table, rows[...], outer, preferred_element_type=jnp.float32
        )

    if scaled:
        gate = jnp.where(at0, gates_ref[0:1, :], 0.0) + jnp.where(at1, gates_ref[1:2, :], 0.0)
        high = gate.astype(jnp.bfloat16)
        low = (gate - high.astype(jnp.float32)).astype(jnp.bfloat16)
        out_ref[...] = (pick(high) + pick(low)).astype(jnp.bfloat16)
    else:
        out_ref[...] = pick(as_bf16(at0 | at1)).astype(jnp.bfloat16)


def combine(me, routes, pieces, experts, capacity, gates=None):
    width = pieces[0].shape[1]
    tokens = routes.shape[1]
    operands = (me, routes) + (() if gates is None else (gates,)) + tuple(pieces)
    return pl.pallas_call(
        functools.partial(combine_kernel, experts, capacity, gates is not None),
        out_shape=jax.ShapeDtypeStruct((tokens, width), jnp.bfloat16),
        in_specs=[pl.BlockSpec(memory_space=pltpu.SMEM)] + whole(len(operands) - 1),
        out_specs=pl.BlockSpec(memory_space=pltpu.VMEM),
        scratch_shapes=[pltpu.VMEM((experts * capacity, width), jnp.bfloat16)],
        compiler_params=params(),
        cost_estimate=pl.CostEstimate(
            flops=2 * tokens * experts * capacity * width,
            bytes_accessed=2 * (tokens * width + experts * capacity * width),
            transcendentals=0,
        ),
        name="combine",
    )(*operands)


def put(out_refs, values, order):
    step, at, places = values.shape[0] // len(order), 0, {}
    for out in out_refs:
        for row in range(0, out.shape[0], step):
            places[at] = (out, row)
            at += 1
    for n, i in enumerate(order):
        out, row = places[i]
        out[row : row + step, :] = values[n * step : (n + 1) * step, :]


def forward_kernel(pieces, outs, order, *refs):
    in_refs = refs[:pieces]
    gate_ref, up_ref, down_ref = refs[pieces : pieces + 3]
    out_refs = refs[pieces + 3 : pieces + 3 + outs]
    rows = refs[-1]
    at = 0
    for ref in in_refs:
        rows[at : at + ref.shape[0], :] = ref[...]
        at += ref.shape[0]
    gate_act = jnp.dot(rows[...], gate_ref[...], preferred_element_type=jnp.float32)
    up_act = jnp.dot(rows[...], up_ref[...], preferred_element_type=jnp.float32)
    hidden = (gate_act * jax.nn.sigmoid(gate_act) * up_act).astype(jnp.bfloat16)
    part = jnp.dot(hidden, down_ref[...], preferred_element_type=jnp.float32).astype(jnp.bfloat16)
    put(out_refs, part, order)


def forward_half(pieces, gate, up, down, outs, order=None):
    n = len(pieces)
    total = sum(piece.shape[0] for piece in pieces)
    width, hidden = gate.shape
    return pl.pallas_call(
        functools.partial(forward_kernel, n, len(outs), order or range(8)),
        out_shape=[jax.ShapeDtypeStruct((rows, width), jnp.bfloat16) for rows in outs],
        in_specs=whole(n + 3),
        out_specs=whole(len(outs)),
        scratch_shapes=[pltpu.VMEM((total, width), jnp.bfloat16)],
        compiler_params=params(),
        cost_estimate=pl.CostEstimate(
            flops=6 * total * width * hidden,
            bytes_accessed=4 * total * width + 6 * width * hidden,
            transcendentals=total * hidden,
        ),
        name="forward_half",
    )(*pieces, gate, up, down)


def backward_kernel(pieces, outs, *refs):
    in_refs = refs[:pieces]
    gate_ref, up_ref, down_ref = refs[pieces : pieces + 3]
    out_refs = refs[pieces + 3 : pieces + 3 + outs]
    hidden_ref, d_gate_ref, d_up_ref, rows, upstream = refs[pieces + 3 + outs :]
    half = in_refs[0].shape[0] // 2
    for i, ref in enumerate(in_refs):
        rows[i * half : (i + 1) * half, :] = ref[0:half, :]
        upstream[i * half : (i + 1) * half, :] = ref[half:, :]
    inner = (((1,), (1,)), ((), ()))
    gate_act = jnp.dot(rows[...], gate_ref[...], preferred_element_type=jnp.float32)
    up_act = jnp.dot(rows[...], up_ref[...], preferred_element_type=jnp.float32)
    d_hidden = lax.dot_general(
        upstream[...], down_ref[...], inner, preferred_element_type=jnp.float32
    )
    sigma = jax.nn.sigmoid(gate_act)
    swish = gate_act * sigma
    hidden_ref[...] = (swish * up_act).astype(jnp.bfloat16)
    d_gate = (d_hidden * up_act * sigma * (1.0 + gate_act * (1.0 - sigma))).astype(jnp.bfloat16)
    d_up = (d_hidden * swish).astype(jnp.bfloat16)
    d_gate_ref[...] = d_gate
    d_up_ref[...] = d_up
    back = lax.dot_general(d_gate, gate_ref[...], inner, preferred_element_type=jnp.float32)
    back = back + lax.dot_general(d_up, up_ref[...], inner, preferred_element_type=jnp.float32)
    back = back.astype(jnp.bfloat16)
    put(out_refs, back, range(8))


def backward_half(pieces, gate, up, down, outs):
    n = len(pieces)
    total = sum(piece.shape[0] for piece in pieces) // 2
    width, hidden = gate.shape
    small = jax.ShapeDtypeStruct((total, hidden), jnp.bfloat16)
    large = jax.ShapeDtypeStruct((total, width), jnp.bfloat16)
    out = pl.pallas_call(
        functools.partial(backward_kernel, n, len(outs)),
        out_shape=[jax.ShapeDtypeStruct((rows, width), jnp.bfloat16) for rows in outs]
        + [small] * 3
        + [large] * 2,
        in_specs=whole(n + 3),
        out_specs=whole(len(outs) + 5),
        compiler_params=params(),
        cost_estimate=pl.CostEstimate(
            flops=10 * total * width * hidden,
            bytes_accessed=10 * total * width + 6 * width * hidden,
            transcendentals=total * hidden,
        ),
        name="backward_half",
    )(*pieces, gate, up, down)
    return out[: len(outs)], out[len(outs) :]


def add_pair(a, b):
    return (a.astype(jnp.float32) + b.astype(jnp.float32)).astype(jnp.bfloat16)


def per_device(
    sent_forward,
    grad_sent,
    saved_inputs,
    routes_forward,
    gates_forward,
    routes_backward,
    gates_backward,
    w_gate,
    w_up,
    w_down,
):
    devices = lax.axis_size("expert")
    experts = devices // 2
    sections = lax.axis_size("section")
    tokens = sent_forward.shape[1]
    chosen = routes_forward.shape[2]
    capacity = 3 * tokens * chosen // (2 * experts)
    me = (lax.axis_index("expert") // 2).astype(jnp.int32).reshape(1)

    def along(array, by):
        return lax.ppermute(array, "section", [(i, (i + by) % sections) for i in range(sections)])

    def to_xor(array, mask):
        return lax.ppermute(array, "expert", [(i, i ^ mask) for i in range(devices)])

    routes_f, gates_f = routes_forward[0].T, gates_forward[0].T
    routes_b, gates_b = routes_backward[0].T, gates_backward[0].T
    weights = w_gate[0, 0], w_up[0, 0], w_down[0, 0]
    span = experts // 8
    group = [list(range(i * span, (i + 1) * span)) for i in range(8)]
    lump = span * capacity
    split = [lump, lump, 2 * lump, 2 * lump, 2 * lump]

    held, met, rounds = {}, [], []

    def after_met(array):
        return lax.optimization_barrier((array, *met))[0] if met else array

    def start(name, arrays, masks):
        held[name] = [
            to_xor(after_met(a), m) if m else a for a, m in zip(arrays, masks, strict=True)
        ]

    def meet(*names):
        met[:] = [a for name in names for a in held[name]]
        rounds.append(list(met))

    def z_start(kind, slots, i):
        start((kind, i), [slots[d] for d in group[i]], [2 * d for d in group[i]])

    def x_start(i):
        start(("x", i), held["b", i], [1] * span)

    def x_join(q, members):
        rows = [a for i in members for a in held["f", i]]
        start(("fx", q), [jnp.concatenate(rows) if len(rows) > 1 else rows[0]], [1])

    def part_start(kind, parts, q):
        start((kind, q), [parts[q + 1]], [1])

    def both_start(i):
        start(("bx", i), [jnp.concatenate([back_other[i], out_other[i]])], [1])

    def give_back(kind, own, i):
        q, first = i // 2, (i % 2) * span
        both = []
        for n in range(span):
            rows = slice((first + n) * capacity, (first + n + 1) * capacity)
            both.append(add_pair(own[q + 1][rows], held[kind + "x", q][0][rows]))
        start((kind, i), both, [2 * d for d in group[i]])

    def give_both(i):
        both = []
        for n in range(span):
            own_rows = slice(n * capacity, (n + 1) * capacity)
            met_rows = slice(lump + n * capacity, lump + (n + 1) * capacity)
            pair = [
                add_pair(back_own[i][own_rows], held["bx", i][0][own_rows]),
                add_pair(out_own[i][own_rows], held["bx", i][0][met_rows]),
            ]
            both.append(jnp.concatenate(pair))
        start(("both", i), both, [2 * d for d in group[i]])
        held["r", i] = [a[:capacity] for a in held["both", i]]
        held["o", i] = [a[capacity:] for a in held["both", i]]

    returned = along(grad_sent, -1)[0]
    arrived = along(sent_forward, 1)[0]
    slots_b = dispatch(me, routes_b, saved_inputs[0], experts, capacity, gates_b, returned)
    slots_b = lax.optimization_barrier((slots_b, arrived))[0]
    slots_f = dispatch(me, routes_f, arrived, experts, capacity)

    z_start("b", slots_b, 0)
    z_start("f", slots_f, 0)
    z_start("b", slots_b, 4)
    x_start(0)
    z_start("b", slots_b, 1)
    x_join(0, [0])
    meet(("b", 4),)
    z_start("b", slots_b, 5)
    meet(("b", 4), ("b", 1), ("x", 0), ("fx", 0))
    x_start(1)
    x_start(4)
    z_start("b", slots_b, 2)
    meet(("b", 5),)
    z_start("b", slots_b, 6)
    meet(("b", 5), ("b", 2), ("x", 1), ("x", 4))
    x_start(2)
    x_start(5)
    z_start("b", slots_b, 3)
    meet(("b", 6),)
    z_start("b", slots_b, 7)
    meet(("b", 6), ("b", 3), ("x", 2), ("x", 5))
    x_start(3)
    x_start(6)
    z_start("f", slots_f, 1)
    meet(("b", 7),)
    z_start("f", slots_f, 4)
    meet(("x", 3), ("x", 6))
    x_start(7)
    meet(("b", 7), ("f", 1), ("x", 3), ("x", 6))
    z_start("f", slots_f, 2)
    back_own, kept_own = backward_half(
        [a for i in range(8) for a in held["b", i]], *weights, split
    )
    meet(("x", 7), ("f", 4), ("f", 2))
    met.append(kept_own[1])
    x_join(1, [1, 2, 4])
    z_start("f", slots_f, 5)
    z_start("f", slots_f, 3)
    back_other, kept_other = backward_half(
        [a for i in range(8) for a in held["x", i]], *weights, split
    )
    meet(("f", 5), ("f", 3), ("fx", 1))
    met.append(kept_other[1])
    part_start("rx", back_other, 2)
    z_start("f", slots_f, 6)
    part_start("rx", back_other, 3)
    z_start("f", slots_f, 7)
    meet(("rx", 2), ("f", 6), ("f", 7), ("rx", 3))
    x_join(2, [3, 5, 6, 7])
    give_back("r", back_own, 4)
    give_back("r", back_own, 5)
    out_own = forward_half([a for i in range(8) for a in held["f", i]], *weights, split)
    meet(("r", 4), ("r", 5), ("fx", 2))
    part_start("rx", back_other, 1)
    give_back("r", back_own, 6)
    give_back("r", back_own, 7)
    other_rows = held["fx", 0] + held["fx", 1] + held["fx", 2]
    out_other = forward_half(other_rows, *weights, split, [0, 1, 2, 4, 3, 5, 6, 7])
    part_start("ox", out_other, 2)
    meet(("rx", 1), ("r", 6), ("r", 7), ("ox", 2))
    part_start("ox", out_other, 3)
    give_back("o", out_own, 4)
    both_start(1)
    give_back("o", out_own, 5)
    give_back("r", back_own, 3)
    meet(("o", 4), ("o", 5))
    give_back("o", out_own, 6)
    meet(("ox", 3), ("bx", 1))
    part_start("ox", out_other, 1)
    meet(("o", 4), ("o", 5), ("ox", 3), ("bx", 1), ("r", 3))
    give_both(1)
    give_back("r", back_own, 2)
    meet(("o", 6),)
    give_back("o", out_own, 7)
    meet(("ox", 1),)
    both_start(0)
    meet(("o", 6), ("ox", 1), ("both", 1), ("r", 2))
    give_back("o", out_own, 2)
    give_back("o", out_own, 3)
    give_both(0)

    outer = (((0,), (0,)), ((), ()))

    def weight_term(a, b, others):
        terms = []
        for kept in (kept_own, kept_other):
            left = lax.optimization_barrier((kept[a], *others))[0]
            terms.append(lax.dot_general(left, kept[b], outer, preferred_element_type=jnp.float32))
        return (terms[0] + terms[1]).astype(jnp.bfloat16)

    grad_gate = weight_term(3, 1, rounds[11])
    grad_up = weight_term(3, 2, rounds[12])
    grad_down = weight_term(0, 4, rounds[13])

    back = [a for i in range(8) for a in held["r", i]]
    out = [a for i in range(8) for a in held["o", i]]
    grad_in = combine(me, routes_b, back, experts, capacity)
    layer_out = combine(me, routes_f, out, experts, capacity, gates_f)
    return (
        layer_out[None],
        grad_in[None],
        grad_gate[None, None],
        grad_up[None, None],
        grad_down[None, None],
    )


def solution(mesh):
    rows = P("section", "expert", None)
    weights = P("section", "expert", None, None)
    return jax.shard_map(
        per_device,
        mesh=mesh,
        in_specs=(rows,) * 7 + (weights,) * 3,
        out_specs=(rows, rows, weights, weights, weights),
        check_vma=False,
    )
```
